32 devices in a mesh: shard: 2 (over x), context: 4 (over z), tensor: 4 (over y, core).
Axes of the slice: x: 2, y: 2, z: 4, core: 2. Of those that a mesh axis runs over, the one named last changes fastest.
Arguments:
- tokens_in: bfloat16 [6, 1536, 1024], P('shard', 'context'), may hold values from -70 to 70
- counts: int32 [6], P('shard'), may hold values from 512 to 1536, as said below
- w_qkv: bfloat16 [1024, 3, 1024], P(('shard', 'context'), None, 'tensor'), may hold values from -0.1875 to 0.1875
- b_qv: bfloat16 [2, 16, 64], P(None, 'tensor', ('shard', 'context')), may hold values from -3 to 3
- w_out: bfloat16 [1024, 1024], P('tensor', ('shard', 'context')), may hold values from -0.5 to 0.5
- b_out: bfloat16 [1024], P(('shard', 'context')), may hold values from -3 to 3
- w_up: bfloat16 [1024, 4096], P(('shard', 'context'), 'tensor'), may hold values from -0.1875 to 0.1875
- b_up: bfloat16 [64, 64], P('tensor', ('shard', 'context')), may hold values from -3 to 3
- w_down: bfloat16 [4096, 1024], P('tensor', ('shard', 'context')), may hold values from -0.09375 to 0.09375
- b_down: bfloat16 [1024], P(('shard', 'context')), may hold values from -3 to 3
- norm1_gain: bfloat16 [1024], P(('shard', 'context')), may hold values from 0.25 to 1.75
- norm1_bias: bfloat16 [1024], P(('shard', 'context')), may hold values from -3 to 3
- norm2_gain: bfloat16 [1024], P(('shard', 'context')), may hold values from 0.25 to 1.75
- norm2_bias: bfloat16 [1024], P(('shard', 'context')), may hold values from -3 to 3
- scale1: bfloat16 [1024], P(('shard', 'context')), may hold values from 0.29882812 to 1.5
- scale2: bfloat16 [1024], P(('shard', 'context')), may hold values from 0.29882812 to 1.5
- cotangent: bfloat16 [6, 1536, 1024], P('shard', 'context'), may hold values from -6 to 6
Outputs:
- output: float32 [6, 1536, 1024], P('shard', 'context')
- input_grad: float32 [6, 1536, 1024], P('shard', 'context')
- g_w_qkv: float32 [1024, 3, 1024], P(('shard', 'context'), None, 'tensor')
- g_b_qv: float32 [2, 16, 64], P(None, 'tensor', ('shard', 'context'))
- g_w_out: float32 [1024, 1024], P('tensor', ('shard', 'context'))
- g_b_out: float32 [1024], P(('shard', 'context'))
- g_w_up: float32 [1024, 4096], P(('shard', 'context'), 'tensor')
- g_b_up: float32 [64, 64], P('tensor', ('shard', 'context'))
- g_w_down: float32 [4096, 1024], P('tensor', ('shard', 'context'))
- g_b_down: float32 [1024], P(('shard', 'context'))
- g_norm1_gain: float32 [1024], P(('shard', 'context'))
- g_norm1_bias: float32 [1024], P(('shard', 'context'))
- g_norm2_gain: float32 [1024], P(('shard', 'context'))
- g_norm2_bias: float32 [1024], P(('shard', 'context'))
- g_scale1: float32 [1024], P(('shard', 'context'))
- g_scale2: float32 [1024], P(('shard', 'context'))
The draws below stay inside these ranges and needn't reach their ends.
Inputs may be any that keep to these rules, and one draw needn't show every extreme that they name: Image i has counts[i] real tokens in its first slots, the rest are padding that is masked as keys; some image fills all 1536 slots.
All inputs are finite; a program needn't handle non-finite values.
Results may differ from the reference program's by a relative error of at most 0.015.
Values may be sent and summed in bfloat16 or wider, within the bound.
No kernel may reach another device: no remote copies, remote signals or barrier semaphores. Data moves between devices by JAX's collectives and lax.ppermute only.
A program may use at most 128 MiB of HBM per device.

```python
import math
import jax
import jax.numpy as jnp
from jax import lax

D = 1024
H = 16
HD = 64
FF = 4096
SEQ = 1536
IMAGES = 6
N_TENSOR = 4


def draw_tokens_in(key, part):
    entry_key, row_key, column_key = jax.random.split(key, 3)
    row_scale = jnp.exp(jax.random.uniform(row_key, (IMAGES, SEQ, 1), minval=0.0, maxval=math.log(10.0)))
    column_scale = jnp.exp(jax.random.uniform(column_key, (1, 1, D), minval=math.log(0.3), maxval=math.log(3.0)))
    entries = jnp.clip(jax.random.normal(entry_key, (IMAGES, SEQ, D)), -4.0, 4.0)
    return (0.5 * entries * row_scale * column_scale).astype(jnp.bfloat16)


def draw_counts(key, part):
    drawn_counts = jax.random.randint(key, (IMAGES,), SEQ // 3, SEQ + 1)
    return drawn_counts.at[0].set(SEQ).astype(jnp.int32)


def level_of(key, extent, shards, least, top_value):
    gain = 1.0
    for position, blocks in shards:
        heights = jax.random.uniform(jax.random.fold_in(jax.random.fold_in(key, 6), position), (blocks,), jnp.float32, least / len(shards), top_value / len(shards))
        gain = gain * jnp.repeat(jnp.exp(heights), extent[position] // blocks).reshape((-1,) + (1,) * (len(extent) - 1 - position))
    return gain


def normal_values(key, extent, spread, most, shards=(), kind=jnp.bfloat16):
    values = jax.random.normal(key, extent, jnp.float32) * spread
    if len(shards) > 0:
        values = level_of(key, extent, shards, -0.22, 0.18) * values
    return jnp.clip(values, min=-most, max=most).astype(kind)


def setup_inputs(seed: int = 0) -> dict:
    splits = jax.random.split(jax.random.key(seed), 18)
    return {
        "tokens_in": draw_tokens_in(jax.random.fold_in(splits[17], 71), 0),
        "counts": draw_counts(jax.random.fold_in(splits[17], 71), 0),
        "w_qkv": normal_values(splits[2], (D, 3, D), D ** -0.5, 0.1875, ((0, 8), (2, 4))),
        "b_qv": normal_values(splits[3], (2, H, HD), 0.5, 3.0, ((1, 4), (2, 8))),
        "w_out": normal_values(splits[4], (D, D), (D // 8) ** -0.5, 0.5, ((0, 4), (1, 8))),
        "b_out": normal_values(splits[5], (D,), 0.5, 3.0, ((0, 8),)),
        "w_up": normal_values(splits[6], (D, FF), D ** -0.5, 0.1875, ((0, 8), (1, 4))),
        "b_up": normal_values(splits[7], (FF // HD, HD), 0.5, 3.0, ((0, 4), (1, 8))),
        "w_down": normal_values(splits[8], (FF, D), FF ** -0.5, 0.09375, ((0, 4), (1, 8))),
        "b_down": normal_values(splits[9], (D,), 0.5, 3.0, ((0, 8),)),
        "norm1_gain": jnp.clip(1.0 + 0.15 * jax.random.normal(splits[10], (D,), jnp.float32), 0.25, 1.75).astype(jnp.bfloat16),
        "norm1_bias": normal_values(splits[11], (D,), 0.5, 3.0, ((0, 8),)),
        "norm2_gain": jnp.clip(1.0 + 0.15 * jax.random.normal(splits[12], (D,), jnp.float32), 0.25, 1.75).astype(jnp.bfloat16),
        "norm2_bias": normal_values(splits[13], (D,), 0.5, 3.0, ((0, 8),)),
        "scale1": jnp.clip(jnp.exp(math.log(1.5) - 1.6133518 * jax.random.uniform(splits[14], (D,), jnp.float32) ** level_of(splits[14], (D,), ((0, 8),), -0.2, 0.2)), 0.29882812, 1.5).astype(jnp.bfloat16),
        "scale2": jnp.clip(jnp.exp(math.log(1.5) - 1.6133518 * jax.random.uniform(splits[15], (D,), jnp.float32) ** level_of(splits[15], (D,), ((0, 8),), -0.2, 0.2)), 0.29882812, 1.5).astype(jnp.bfloat16),
        "cotangent": normal_values(splits[16], (IMAGES, SEQ, D), 1.0, 6.0, ((0, 2), (1, 4))),
    }


eps_norm = 1e-06
masked_score = -1e+30
root_half = 0.7071067811865476
inv_root_two_pi = 0.3989422804014327

def layer_norm(values, norm_gain, norm_shift):
    average = lax.optimization_barrier(jnp.mean(values, axis=-1, keepdims=True))
    centred = values - average
    variance = lax.optimization_barrier(jnp.mean(centred * centred, axis=-1, keepdims=True))
    inv_std = lax.rsqrt(variance + eps_norm)
    normed = centred * inv_std
    return (normed * norm_gain + norm_shift, normed, inv_std)

def norm_back(grad_in, normed, inv_std):
    first_mean = lax.optimization_barrier(jnp.mean(grad_in, axis=-1, keepdims=True))
    second_mean = lax.optimization_barrier(jnp.mean(grad_in * normed, axis=-1, keepdims=True))
    return inv_std * (grad_in - first_mean - normed * second_mean)

def gelu_exact(values):
    return 0.5 * values * (1.0 + lax.erf(values * root_half))

def gelu_slope(values):
    return 0.5 * (1.0 + lax.erf(values * root_half)) + values * inv_root_two_pi * jnp.exp(-0.5 * values * values)

def group_partials(left, right, groups):
    row_count = left.shape[0]
    left_parts = left.astype(jnp.float32).reshape(row_count, groups, -1)
    right_parts = right.astype(jnp.float32).reshape(groups, -1, right.shape[1])
    partial_value = jnp.einsum('rgk,gkn->grn', left_parts, right_parts, precision=lax.Precision.HIGHEST)
    rounded = lax.optimization_barrier(partial_value.astype(jnp.bfloat16))
    return lax.optimization_barrier(jnp.sum(rounded.astype(jnp.float32), axis=0))

def attend_all(queries, key_rows, value_rows, key_valid):
    length = queries.shape[0]
    block_rows = min(512, length)
    blocks = length // block_rows
    score_scale = HD ** (-0.5)
    key_wide = key_rows.astype(jnp.float32)
    value_wide = value_rows.astype(jnp.float32)

    def one_block(query_block):
        scores = jnp.einsum('qhd,khd->hqk', query_block.astype(jnp.float32), key_wide, precision=lax.Precision.HIGHEST) * score_scale
        scores = jnp.where(key_valid[None, None, :], scores, masked_score)
        highest = lax.optimization_barrier(jnp.max(scores, axis=2, keepdims=True))
        exponent = jnp.exp(scores - highest)
        denominator = lax.optimization_barrier(jnp.sum(exponent, axis=2, keepdims=True))
        weights_low = (exponent / denominator).astype(jnp.bfloat16)
        mixture = jnp.einsum('hqk,khd->qhd', weights_low.astype(jnp.float32), value_wide, precision=lax.Precision.HIGHEST)
        return (mixture.astype(jnp.bfloat16), (highest + jnp.log(denominator))[:, :, 0])
    mixture, log_total = lax.map(one_block, queries.reshape(blocks, block_rows, H, HD))
    return (mixture.reshape(length, H * HD), log_total)

def attend_back(queries, key_rows, value_rows, mixture, mixture_grad, log_total, key_valid):
    length = queries.shape[0]
    block_rows = min(512, length)
    blocks = length // block_rows
    score_scale = HD ** (-0.5)
    key_wide = key_rows.astype(jnp.float32)
    value_wide = value_rows.astype(jnp.float32)
    grad_heads = mixture_grad.reshape(length, H, HD)
    delta_sum = lax.optimization_barrier(jnp.sum(mixture.reshape(length, H, HD).astype(jnp.float32) * grad_heads.astype(jnp.float32), axis=2))

    def one_block(running, block_in):
        key_grad, value_grad = running
        query_block, grad_block, log_block, delta_block = block_in
        query_wide = query_block.astype(jnp.float32)
        grad_wide = grad_block.astype(jnp.float32)
        scores = jnp.einsum('qhd,khd->hqk', query_wide, key_wide, precision=lax.Precision.HIGHEST) * score_scale
        scores = jnp.where(key_valid[None, None, :], scores, masked_score)
        probs = jnp.exp(scores - log_block[:, :, None])
        probs_low = probs.astype(jnp.bfloat16).astype(jnp.float32)
        value_grad = value_grad + jnp.einsum('hqk,qhd->khd', probs_low, grad_wide, precision=lax.Precision.HIGHEST)
        weight_grad = jnp.einsum('qhd,khd->hqk', grad_wide, value_wide, precision=lax.Precision.HIGHEST)
        score_grad = (probs * (weight_grad - jnp.transpose(delta_block)[:, :, None])).astype(jnp.bfloat16).astype(jnp.float32)
        query_grad = (jnp.einsum('hqk,khd->qhd', score_grad, key_wide, precision=lax.Precision.HIGHEST) * score_scale).astype(jnp.bfloat16)
        key_grad = key_grad + jnp.einsum('hqk,qhd->khd', score_grad, query_wide, precision=lax.Precision.HIGHEST) * score_scale
        return ((key_grad, value_grad), query_grad)
    zero_grad = jnp.zeros((length, H, HD), jnp.float32)
    block_inputs = (queries.reshape(blocks, block_rows, H, HD), grad_heads.reshape(blocks, block_rows, H, HD), log_total, delta_sum.reshape(blocks, block_rows, H))
    (key_grad, value_grad), query_grads = lax.scan(one_block, (zero_grad, zero_grad), block_inputs)
    return jnp.stack([query_grads.reshape(length, H * HD), key_grad.astype(jnp.bfloat16).reshape(length, H * HD), value_grad.astype(jnp.bfloat16).reshape(length, H * HD)], axis=1)

def reference(tokens_in, counts, w_qkv, b_qv, w_out, b_out, w_up, b_up, w_down, b_down, norm1_gain, norm1_bias, norm2_gain, norm2_bias, scale1, scale2, cotangent):
    wqkv_flat = w_qkv.reshape(D, 3 * D)
    bias_rows = b_qv.astype(jnp.float32).reshape(2, D)
    qkv_bias = jnp.stack([bias_rows[0], jnp.zeros((D,), jnp.float32), bias_rows[1]])
    gain_one = norm1_gain.astype(jnp.float32)
    bias_one = norm1_bias.astype(jnp.float32)
    gain_two = norm2_gain.astype(jnp.float32)
    bias_two = norm2_bias.astype(jnp.float32)
    layer_scale1 = scale1.astype(jnp.float32)
    layer_scale2 = scale2.astype(jnp.float32)
    bout_wide = b_out.astype(jnp.float32)
    bup_wide = b_up.astype(jnp.float32).reshape(FF)
    bdown_wide = b_down.astype(jnp.float32)

    def image_step(running, item):
        tokens, upstream_low, image_count = item
        residual_in = tokens.astype(jnp.float32)
        key_valid = jnp.arange(SEQ) < image_count
        norm_out1, normed1, inv_std1 = layer_norm(residual_in, gain_one, bias_one)
        norm_low1 = norm_out1.astype(jnp.bfloat16)
        projected = jnp.dot(norm_low1, wqkv_flat, preferred_element_type=jnp.float32).reshape(SEQ, 3, D) + qkv_bias
        packed = projected.astype(jnp.bfloat16)
        queries = packed[:, 0].reshape(SEQ, H, HD)
        key_rows = packed[:, 1].reshape(SEQ, H, HD)
        value_rows = packed[:, 2].reshape(SEQ, H, HD)
        mixture, log_total = attend_all(queries, key_rows, value_rows, key_valid)
        attn_branch = group_partials(mixture, w_out, N_TENSOR) + bout_wide
        middle = residual_in + layer_scale1 * attn_branch
        norm_out2, normed2, inv_std2 = layer_norm(middle, gain_two, bias_two)
        norm_low2 = norm_out2.astype(jnp.bfloat16)
        hidden_pre = jnp.dot(norm_low2, w_up, preferred_element_type=jnp.float32) + bup_wide
        hidden_act = gelu_exact(hidden_pre).astype(jnp.bfloat16)
        mlp_branch = group_partials(hidden_act, w_down, N_TENSOR) + bdown_wide
        result = middle + layer_scale2 * mlp_branch
        upstream = upstream_low.astype(jnp.float32)
        grad_scale2 = lax.optimization_barrier(jnp.sum(upstream * mlp_branch, axis=0))
        branch_wide = layer_scale2 * upstream
        grad_bdown = lax.optimization_barrier(jnp.sum(branch_wide, axis=0))
        branch_grad = branch_wide.astype(jnp.bfloat16)
        grad_wdown = jnp.dot(hidden_act.T, branch_grad, preferred_element_type=jnp.float32)
        pre_grad = (jnp.dot(branch_grad, w_down.T, preferred_element_type=jnp.float32) * gelu_slope(hidden_pre)).astype(jnp.bfloat16)
        grad_wup = jnp.dot(norm_low2.T, pre_grad, preferred_element_type=jnp.float32)
        grad_bup = lax.optimization_barrier(jnp.sum(pre_grad.astype(jnp.float32), axis=0)).reshape(FF // HD, HD)
        norm2_grad = group_partials(pre_grad, w_up.T, N_TENSOR)
        grad_gain2 = lax.optimization_barrier(jnp.sum(norm2_grad * normed2, axis=0))
        grad_bias2 = lax.optimization_barrier(jnp.sum(norm2_grad, axis=0))
        middle_grad = upstream + norm_back(norm2_grad * gain_two, normed2, inv_std2)
        grad_scale1 = lax.optimization_barrier(jnp.sum(middle_grad * attn_branch, axis=0))
        proj_wide = layer_scale1 * middle_grad
        grad_bout = lax.optimization_barrier(jnp.sum(proj_wide, axis=0))
        proj_grad = proj_wide.astype(jnp.bfloat16)
        grad_wout = jnp.dot(mixture.T, proj_grad, preferred_element_type=jnp.float32)
        mixture_grad = jnp.dot(proj_grad, w_out.T, preferred_element_type=jnp.float32).astype(jnp.bfloat16)
        qkv_grad = attend_back(queries, key_rows, value_rows, mixture, mixture_grad, log_total, key_valid)
        grad_wqkv = jnp.dot(norm_low1.T, qkv_grad.reshape(SEQ, 3 * D), preferred_element_type=jnp.float32).reshape(D, 3, D)
        summed_qkv = lax.optimization_barrier(jnp.sum(qkv_grad.astype(jnp.float32), axis=0))
        grad_bqv = jnp.stack([summed_qkv[0], summed_qkv[2]]).reshape(2, H, HD)
        grad_parts = qkv_grad.astype(jnp.float32).reshape(SEQ, 3, N_TENSOR, D // N_TENSOR)
        weight_parts = w_qkv.astype(jnp.float32).reshape(D, 3, N_TENSOR, D // N_TENSOR)
        partial_value = jnp.einsum('scge,dcge->gsd', grad_parts, weight_parts, precision=lax.Precision.HIGHEST)
        rounded = lax.optimization_barrier(partial_value.astype(jnp.bfloat16))
        norm1_grad = lax.optimization_barrier(jnp.sum(rounded.astype(jnp.float32), axis=0))
        grad_gain1 = lax.optimization_barrier(jnp.sum(norm1_grad * normed1, axis=0))
        grad_bias1 = lax.optimization_barrier(jnp.sum(norm1_grad, axis=0))
        input_grad = middle_grad + norm_back(norm1_grad * gain_one, normed1, inv_std1)
        fresh = (grad_wqkv, grad_bqv, grad_wout, grad_bout, grad_wup, grad_bup, grad_wdown, grad_bdown, grad_gain1, grad_bias1, grad_gain2, grad_bias2, grad_scale1, grad_scale2)
        running = jax.tree.map(jnp.add, running, fresh)
        return (running, (result, input_grad))
    start = (jnp.zeros((D, 3, D), jnp.float32), jnp.zeros((2, H, HD), jnp.float32), jnp.zeros((D, D), jnp.float32), jnp.zeros((D,), jnp.float32), jnp.zeros((D, FF), jnp.float32), jnp.zeros((FF // HD, HD), jnp.float32), jnp.zeros((FF, D), jnp.float32), jnp.zeros((D,), jnp.float32), jnp.zeros((D,), jnp.float32), jnp.zeros((D,), jnp.float32), jnp.zeros((D,), jnp.float32), jnp.zeros((D,), jnp.float32), jnp.zeros((D,), jnp.float32), jnp.zeros((D,), jnp.float32))
    grads, (output, input_grad) = lax.scan(image_step, start, (tokens_in, cotangent, counts.astype(jnp.int32)))
    return (output, input_grad, grads[0], grads[1], grads[2], grads[3], grads[4], grads[5], grads[6], grads[7], grads[8], grads[9], grads[10], grads[11], grads[12], grads[13])
```

```python
import functools

import jax
import jax.numpy as jnp
from jax import lax
from jax.experimental import pallas as pl
from jax.experimental.pallas import tpu as pltpu
from jax.sharding import PartitionSpec as P

HD = 64
LANES = 128
CORES = 2

eps_norm = 1e-06
masked_score = -1e30
root_half = 0.7071067811865476
inv_root_two_pi = 0.3989422804014327
score_scale = HD ** (-0.5)

bf16 = jnp.bfloat16
f32 = jnp.float32
NN = (((1,), (0,)), ((), ()))
NT = (((1,), (1,)), ((), ()))
TN = (((0,), (0,)), ((), ()))


def mm(left, right, dims=NN):
    return lax.dot_general(left, right, dims, preferred_element_type=f32)


def layer_norm(values, norm_gain, norm_shift):
    average = jnp.mean(values, axis=-1, keepdims=True)
    centred = values - average
    variance = jnp.mean(centred * centred, axis=-1, keepdims=True)
    inv_std = lax.rsqrt(variance + eps_norm)
    normed = centred * inv_std
    return (normed * norm_gain + norm_shift, normed, inv_std)


def norm_back(grad_in, normed, inv_std):
    first_mean = jnp.mean(grad_in, axis=-1, keepdims=True)
    second_mean = jnp.mean(grad_in * normed, axis=-1, keepdims=True)
    return inv_std * (grad_in - first_mean - normed * second_mean)


def low_lanes(shape):
    return lax.broadcasted_iota(jnp.int32, shape, 1) < HD


def swap(values):
    return pltpu.roll(values, HD, 1)


def fold(wide):
    half = wide.shape[0] // 2
    return wide[:half] + swap(wide[half:])


def unfold(folded):
    low = low_lanes(folded.shape)
    return jnp.concatenate(
        [jnp.where(low, folded, 0.0), jnp.where(low, swap(folded), 0.0)], axis=0
    )


def qkv_kernel(images, z_ref, x_ref, gain_ref, shift_ref, bias_ref, *refs):
    weights, outs, norm_ref, scratch = refs[:4], refs[4:12], refs[12], refs[13]
    context = len(outs) // 2
    z = z_ref[0]
    rows = x_ref.shape[0] // images
    half = rows // 2
    norm_out, _, _ = layer_norm(x_ref[...].astype(f32), gain_ref[...], shift_ref[...])
    norm_low = norm_out.astype(bf16)
    norm_ref[...] = norm_low
    low = low_lanes((rows, LANES))
    low_half = low_lanes((half, LANES))
    for piece in range(4):
        block = mm(norm_low, weights[piece][...]) + bias_ref[piece : piece + 1, :]
        for image in range(images):
            part = block[image * rows : (image + 1) * rows]
            query, key, value = part[:, :LANES], part[:, LANES : 2 * LANES], part[:, 2 * LANES :]
            head = piece * 2
            scratch[head, image, :rows] = jnp.where(low, query, swap(key)).astype(bf16)
            scratch[head + 1, image, :rows] = jnp.where(low, swap(query), key).astype(bf16)
            scratch[head, image, rows:] = jnp.where(
                low_half, value[:half], swap(value[half:])
            ).astype(bf16)
            scratch[head + 1, image, rows:] = jnp.where(
                low_half, swap(value[:half]), value[half:]
            ).astype(bf16)
    for slot in range(2 * context):
        owner = slot // context * context + lax.rem(z + slot % context, context)
        outs[slot][...] = scratch[owner]


def attend_kernel(count_ref, pos_ref, *refs):
    blocks = (len(refs) - 3) // 2
    packs, outs, log_ref, keys, values = (
        refs[:blocks],
        refs[blocks : 2 * blocks],
        refs[2 * blocks],
        refs[2 * blocks + 1],
        refs[2 * blocks + 2],
    )
    rows = packs[0].shape[1] * 2 // 3
    low = low_lanes((rows, LANES))
    for j in range(blocks):
        pack = packs[j][0].astype(f32)
        keys[j * rows : (j + 1) * rows] = jnp.where(low, swap(pack[:rows]), 0.0).astype(bf16)
        values[j * rows : (j + 1) * rows] = unfold(pack[rows:]).astype(bf16)
    valid = pos_ref[...] < count_ref[pl.program_id(0)]
    for j in range(blocks):
        query = packs[j][0, :rows] * bf16(score_scale)
        scores = jnp.where(valid, mm(query, keys[...], NT), masked_score)
        highest = jnp.max(scores, axis=1, keepdims=True)
        exponent = jnp.exp(scores - highest)
        total = jnp.sum(exponent, axis=1, keepdims=True)
        mixed = mm(exponent.astype(bf16), values[...]) / total
        outs[j][0] = fold(mixed).astype(bf16)
        log_ref[0, j * rows : (j + 1) * rows] = highest + jnp.log(total)


def attend_back_kernel(count_ref, pos_ref, log_ref, *refs):
    blocks = (len(refs) - 4) // 4
    packs, mixes, grads, outs = (refs[i * blocks : (i + 1) * blocks] for i in range(4))
    keys, values, sums, query_grads = refs[4 * blocks :]
    rows = packs[0].shape[1] * 2 // 3
    half = rows // 2
    low = low_lanes((rows, LANES))
    low_half = low_lanes((half, LANES))
    for j in range(blocks):
        pack = packs[j][0].astype(f32)
        keys[j * rows : (j + 1) * rows] = jnp.where(low, swap(pack[:rows]), 0.0).astype(bf16)
        values[j * rows : (j + 1) * rows] = unfold(pack[rows:]).astype(bf16)
    valid = pos_ref[...] < count_ref[pl.program_id(0)]
    for j in range(blocks):
        query = packs[j][0, :rows] * bf16(score_scale)
        grad_wide = unfold(grads[j][0].astype(f32))
        mix_wide = unfold(mixes[j][0].astype(f32))
        delta = jnp.sum(grad_wide * mix_wide, axis=1, keepdims=True)
        grad = grad_wide.astype(bf16)
        scores = jnp.where(valid, mm(query, keys[...], NT), masked_score)
        probs = jnp.exp(scores - log_ref[0, j * rows : (j + 1) * rows])
        weight_grad = mm(grad, values[...], NT)
        score_grad = (probs * (weight_grad - delta)).astype(bf16)
        query_grads[j] = mm(score_grad, keys[...]) * score_scale
        query_t = jnp.transpose(query.astype(f32))[:HD].astype(bf16)
        grad_t = jnp.transpose(grad_wide)[:HD].astype(bf16)
        key_part = mm(query_t, score_grad)
        value_part = mm(grad_t, probs.astype(bf16))
        if j == 0:
            sums[:HD] = key_part
            sums[HD:] = value_part
        else:
            sums[:HD] = sums[:HD] + key_part
            sums[HD:] = sums[HD:] + value_part
    for j in range(blocks):
        both = jnp.transpose(sums[:, j * rows : (j + 1) * rows])
        outs[j][0, :rows] = jnp.where(low, query_grads[j], swap(both)).astype(bf16)
        outs[j][0, rows:] = jnp.where(low_half, swap(both[:half]), both[half:]).astype(bf16)


def gather_heads(z, folded, scratch, mixed_ref):
    context = len(folded) // 2
    images, half, _ = folded[0].shape
    rows = 2 * half
    for slot in range(2 * context):
        owner = slot // context * context + lax.rem(z + slot % context, context)
        scratch[owner] = folded[slot][...]
    low = low_lanes((half, LANES))
    for pair in range(context):
        for image in range(images):
            first = scratch[2 * pair, image].astype(f32)
            second = scratch[2 * pair + 1, image].astype(f32)
            start = image * rows
            columns = slice(pair * LANES, (pair + 1) * LANES)
            mixed_ref[start : start + half, columns] = jnp.where(
                low, first, swap(second)
            ).astype(bf16)
            mixed_ref[start + half : start + rows, columns] = jnp.where(
                low, swap(first), second
            ).astype(bf16)


def project_kernel(z_ref, *refs):
    folded, weights, mixed_ref, part_ref, scratch = refs[:8], refs[8:12], refs[12], refs[13], refs[14]
    gather_heads(z_ref[0], folded, scratch, mixed_ref)
    weight = jnp.concatenate([w[...] for w in weights], axis=1)
    part_ref[...] = mm(mixed_ref[...], weight, NT).astype(bf16)


def project_back_kernel(images, z_ref, grad_ref, *refs):
    weights, outs, scratch = refs[:4], refs[4:12], refs[12]
    context = len(outs) // 2
    z = z_ref[0]
    rows = grad_ref.shape[0] // images
    half = rows // 2
    low = low_lanes((half, LANES))
    weight = jnp.concatenate([w[...] for w in weights], axis=1)
    wide = mm(grad_ref[...], weight)
    for pair in range(4):
        for image in range(images):
            block = wide[image * rows : (image + 1) * rows, pair * LANES : (pair + 1) * LANES]
            first, second = block[:half], block[half:]
            scratch[2 * pair, image] = jnp.where(low, first, swap(second)).astype(bf16)
            scratch[2 * pair + 1, image] = jnp.where(low, swap(first), second).astype(bf16)
    for slot in range(2 * context):
        owner = slot // context * context + lax.rem(z + slot % context, context)
        outs[slot][...] = scratch[owner]


def qkv_back_kernel(z_ref, *refs):
    packs, weights, grads, part_ref, scratch = (
        refs[:8],
        refs[8:12],
        refs[12:16],
        refs[16],
        refs[17],
    )
    z = z_ref[0]
    context = len(packs) // 2
    images = packs[0].shape[0]
    rows = packs[0].shape[1] * 2 // 3
    half = rows // 2
    for slot in range(2 * context):
        owner = slot // context * context + lax.rem(z + slot % context, context)
        scratch[owner] = packs[slot][...]
    low = low_lanes((rows, LANES))
    low_half = low_lanes((half, LANES))
    total = None
    for piece in range(4):
        for image in range(images):
            first = scratch[2 * piece, image].astype(f32)
            second = scratch[2 * piece + 1, image].astype(f32)
            start = image * rows
            grads[piece][start : start + rows, :LANES] = jnp.where(
                low, first[:rows], swap(second[:rows])
            ).astype(bf16)
            grads[piece][start : start + rows, LANES : 2 * LANES] = jnp.where(
                low, swap(first[:rows]), second[:rows]
            ).astype(bf16)
            grads[piece][start : start + half, 2 * LANES :] = jnp.where(
                low_half, first[rows:], swap(second[rows:])
            ).astype(bf16)
            grads[piece][start + half : start + rows, 2 * LANES :] = jnp.where(
                low_half, swap(first[rows:]), second[rows:]
            ).astype(bf16)
        part = mm(grads[piece][...], weights[piece][...], NT)
        total = part if total is None else total + part
    part_ref[...] = total.astype(bf16)


def vmem():
    return pl.BlockSpec(memory_space=pltpu.VMEM)


def smem():
    return pl.BlockSpec(memory_space=pltpu.SMEM)


def shaped(shape, dtype):
    return jax.ShapeDtypeStruct(shape, dtype)


def per_device(sizes, *args):
    (
        tokens_in,
        counts,
        w_qkv,
        b_qv,
        w_out,
        b_out,
        w_up,
        b_up,
        w_down,
        b_down,
        norm1_gain,
        norm1_bias,
        norm2_gain,
        norm2_bias,
        scale1,
        scale2,
        cotangent,
    ) = args
    n_shard, n_context, n_tensor = sizes
    images, row_count, width = tokens_in.shape
    piece_rows = w_qkv.shape[0]
    n_y = n_tensor // CORES
    rows = row_count // n_y
    half = rows // 2
    tokens = images * rows
    x = lax.axis_index("shard")
    z = lax.axis_index("context")
    y = lax.axis_index("tensor") // CORES
    z_arg = z.astype(jnp.int32).reshape(1)
    blocks = n_y * n_context

    def send(value, axis, step):
        size = {"shard": n_shard, "context": n_context}[axis]
        return lax.ppermute(value, axis, [(i, (i + step) % size) for i in range(size)])

    def across(value):
        return lax.ppermute(value, "tensor", [(i, i ^ CORES) for i in range(n_tensor)])

    def partner(value):
        return lax.ppermute(value, "tensor", [(i, i ^ 1) for i in range(n_tensor)])

    def hand_over(values, back):
        out = [values[0]]
        for slot in range(1, blocks):
            jy, jz = slot // n_context, slot % n_context
            step = -jz if back else jz
            pairs = [
                (i * n_tensor + t, (i + step) % n_context * n_tensor + (t ^ (jy * CORES)))
                for i in range(n_context)
                for t in range(n_tensor)
            ]
            out.append(lax.ppermute(values[slot], ("context", "tensor"), pairs))
        return out

    def along_context(value):
        parts = [value] + [send(value, "context", j) for j in range(1, n_context)]
        return jnp.concatenate(parts, axis=0)

    def along_shard(value):
        parts = [value] + [send(value, "shard", j) for j in range(1, n_shard)]
        return jnp.concatenate(parts, axis=0)

    def fetch(piece):
        middle = piece.shape[1] // 2
        whole = along_context(piece)
        first, second = whole[:, :middle], whole[:, middle:]
        own_a = along_shard(first)
        far_b = across(second)
        own_b = along_shard(second)
        other_a = across(own_a)
        other_b = along_shard(far_b)
        return [own_a, own_b, other_a, other_b]

    def add(left, right):
        return left.astype(f32) + right.astype(f32)

    def over_shard(value):
        part = value.reshape((n_shard, -1) + value.shape[1:])
        total = part[0].astype(f32)
        for j in range(1, n_shard):
            total = total + send(part[j], "shard", -j).astype(f32)
        return total

    def over_context(value):
        part = value.reshape((n_context, -1) + value.shape[1:])
        total = part[0].astype(f32)
        for j in range(1, n_context):
            total = total + send(part[j], "context", -j).astype(f32)
        return total

    def share(own_a, own_b, other_a, other_b):
        sum_a = over_shard(add(own_a, across(other_a)).astype(bf16))
        near, far = over_shard(own_b).astype(bf16), over_shard(other_b).astype(bf16)
        sum_b = add(near, across(far))
        return over_context(jnp.concatenate([sum_a, sum_b], axis=1).astype(bf16))

    vectors = [b_out, b_down, norm1_gain, norm1_bias, norm2_gain, norm2_bias, scale1, scale2]
    n_vec, n_qv, n_up = len(vectors) * piece_rows, b_qv.size, b_up.size
    small_size = -(-(n_vec + n_qv + n_up) // 2048) * 2048
    small = jnp.concatenate(
        vectors
        + [b_qv.reshape(-1), b_up.reshape(-1)]
        + [jnp.zeros((small_size - n_vec - n_qv - n_up,), bf16)]
    ).reshape(-1, LANES)
    shards = n_shard * n_context
    small_own = along_shard(along_context(small))
    small_other = across(small_own)
    small_own = small_own.reshape(shards, small_size)
    small_other = small_other.reshape(shards, small_size)
    position = jnp.arange(shards)
    relative_of = (x - position // n_context) % n_shard * n_context + (
        z - position % n_context
    ) % n_context
    actual_of = (x - position // n_context) % n_shard * n_context + (
        z - position % n_context
    ) % n_context

    wide = [
        small_own[:, i * piece_rows : (i + 1) * piece_rows].astype(f32).reshape(1, width)
        for i in range(len(vectors))
    ]
    bout, bdown, gain1, shift1, gain2, shift2, layer_scale1, layer_scale2 = wide
    both = jnp.take(jnp.stack([small_own, small_other]), relative_of, axis=1).astype(f32)
    n_qv_last, n_up_last = b_qv.shape[2], b_up.shape[1]
    qv_all = both[:, :, n_vec : n_vec + n_qv].reshape((2, shards) + b_qv.shape)
    qv_all = qv_all.transpose(0, 2, 3, 1, 4).reshape(2, 2, -1, 2 * HD)
    qkv_bias = jnp.stack([qv_all[:, 0], jnp.zeros_like(qv_all[:, 0]), qv_all[:, 1]], axis=2)
    qkv_bias = qkv_bias.reshape(4, 3 * LANES)
    up_all = both[:, :, n_vec + n_qv : n_vec + n_qv + n_up].reshape((2, shards) + b_up.shape)
    bup = up_all.transpose(0, 2, 1, 3).reshape(1, -1)

    columns = w_qkv.shape[2]
    middle = columns // 2
    qkv_piece = jnp.concatenate(
        [w_qkv[:, :, :middle].reshape(piece_rows, -1), w_qkv[:, :, middle:].reshape(piece_rows, -1)],
        axis=1,
    )
    wqkv = fetch(qkv_piece)
    wout = fetch(w_out.T)
    wup = jnp.concatenate(fetch(w_up), axis=1)
    wdown = jnp.concatenate(fetch(w_down.T), axis=1)

    feature = jnp.arange(width)
    target = actual_of[feature // piece_rows] * piece_rows + feature % piece_rows
    turn = (feature[:, None] == target[None, :]).astype(bf16)

    def own_rows(array):
        part = lax.dynamic_slice_in_dim(array, y * rows, rows, 1).reshape(tokens, width)
        return mm(part, turn).astype(bf16)

    def whole_rows(value):
        low = mm(value.astype(bf16), turn, NT).astype(bf16)
        other = across(low)
        low, other = (v.reshape(images, rows, width) for v in (low, other))
        out = jnp.zeros((images, row_count, width), bf16)
        out = lax.dynamic_update_slice_in_dim(out, low, y * rows, 1)
        out = lax.dynamic_update_slice_in_dim(out, other, (1 - y) * rows, 1)
        return out.astype(f32)

    residual_low = own_rows(tokens_in)
    upstream_low = own_rows(cotangent)
    residual_in = residual_low.astype(f32)
    upstream = upstream_low.astype(f32)

    pack_rows = rows + half
    packed = pl.pallas_call(
        functools.partial(qkv_kernel, images),
        name="qkv",
        in_specs=[smem()] + [vmem()] * 8,
        out_specs=[vmem()] * (blocks + 1),
        out_shape=[shaped((images, pack_rows, LANES), bf16)] * blocks
        + [shaped((tokens, width), bf16)],
        scratch_shapes=[pltpu.VMEM((blocks, images, pack_rows, LANES), bf16)],
    )(z_arg, residual_low, gain1, shift1, qkv_bias, *wqkv)
    norm_low1 = packed[blocks]
    packs = hand_over(packed[:blocks], False)

    slot = jnp.arange(blocks)
    source = (z - slot % n_context) % n_context * row_count + (y ^ (slot // n_context)) * rows
    key_place = (source[:, None] + jnp.arange(rows)[None, :]).reshape(1, -1).astype(jnp.int32)
    length = blocks * rows
    pack_spec = pl.BlockSpec((1, pack_rows, LANES), lambda i: (i, 0, 0))
    fold_spec = pl.BlockSpec((1, half, LANES), lambda i: (i, 0, 0))
    pos_spec = pl.BlockSpec((1, length), lambda i: (0, 0))
    log_spec = pl.BlockSpec((1, length, 1), lambda i: (i, 0, 0))
    attended = pl.pallas_call(
        attend_kernel,
        name="attend",
        grid=(images,),
        in_specs=[smem(), pos_spec] + [pack_spec] * blocks,
        out_specs=[fold_spec] * blocks + [log_spec],
        out_shape=[shaped((images, half, LANES), bf16)] * blocks
        + [shaped((images, length, 1), f32)],
        scratch_shapes=[pltpu.VMEM((length, LANES), bf16)] * 2,
    )(counts, key_place, *packs)
    mixes, log_total = attended[:blocks], attended[blocks]
    folded = hand_over(mixes, True)

    mixture, proj_part = pl.pallas_call(
        project_kernel,
        name="project",
        in_specs=[smem()] + [vmem()] * (blocks + 4),
        out_specs=[vmem()] * 2,
        out_shape=[
            shaped((tokens, blocks * HD), bf16),
            shaped((tokens, width), bf16),
        ],
        scratch_shapes=[pltpu.VMEM((blocks, images, half, LANES), bf16)],
    )(z_arg, *folded, *wout)

    attn_branch = add(proj_part, partner(proj_part)) + bout
    middle_rows = residual_in + layer_scale1 * attn_branch
    norm_out2, normed2, inv_std2 = layer_norm(middle_rows, gain2, shift2)
    norm_low2 = norm_out2.astype(bf16)
    hidden_pre = mm(norm_low2, wup) + bup
    erf_term = 0.5 * (1.0 + lax.erf(hidden_pre * root_half))
    hidden_act = (hidden_pre * erf_term).astype(bf16)
    down_part = mm(hidden_act, wdown, NT).astype(bf16)
    branch_wide = layer_scale2 * upstream
    branch_grad = branch_wide.astype(bf16)
    slope = erf_term + hidden_pre * inv_root_two_pi * jnp.exp(-0.5 * hidden_pre * hidden_pre)
    pre_grad = (mm(branch_grad, wdown) * slope).astype(bf16)
    norm2_part = mm(pre_grad, wup, NT).astype(bf16)
    norm2_grad = add(norm2_part, partner(norm2_part))
    mlp_branch = add(down_part, partner(down_part)) + bdown
    result = middle_rows + layer_scale2 * mlp_branch

    grad_scale2 = jnp.sum(upstream * mlp_branch, axis=0)
    grad_bdown = jnp.sum(branch_wide, axis=0)
    grad_bup = jnp.sum(pre_grad.astype(f32), axis=0)
    grad_gain2 = jnp.sum(norm2_grad * normed2, axis=0)
    grad_shift2 = jnp.sum(norm2_grad, axis=0)
    middle_grad = upstream + norm_back(norm2_grad * gain2, normed2, inv_std2)
    grad_scale1 = jnp.sum(middle_grad * attn_branch, axis=0)
    proj_wide = layer_scale1 * middle_grad
    grad_bout = jnp.sum(proj_wide, axis=0)
    proj_grad = proj_wide.astype(bf16)

    mix_grads = pl.pallas_call(
        functools.partial(project_back_kernel, images),
        name="project_back",
        in_specs=[smem()] + [vmem()] * 5,
        out_specs=[vmem()] * blocks,
        out_shape=[shaped((images, half, LANES), bf16)] * blocks,
        scratch_shapes=[pltpu.VMEM((blocks, images, half, LANES), bf16)],
    )(z_arg, proj_grad, *wout)
    mix_grads = hand_over(mix_grads, False)

    pack_grads = pl.pallas_call(
        attend_back_kernel,
        name="attend_back",
        grid=(images,),
        in_specs=[smem(), pos_spec, log_spec]
        + [pack_spec] * blocks
        + [fold_spec] * (2 * blocks),
        out_specs=[pack_spec] * blocks,
        out_shape=[shaped((images, pack_rows, LANES), bf16)] * blocks,
        scratch_shapes=[pltpu.VMEM((length, LANES), bf16)] * 2
        + [pltpu.VMEM((2 * HD, length), f32), pltpu.VMEM((blocks, rows, LANES), f32)],
    )(counts, key_place, log_total, *packs, *mixes, *mix_grads)
    pack_grads = hand_over(pack_grads, True)

    def pieces(left, right, count):
        whole = mm(left, right, TN).astype(bf16)
        size = whole.shape[1] // count
        return [whole[:, i * size : (i + 1) * size] for i in range(count)]

    grad_wdown = share(*pieces(branch_grad, hidden_act, 4)).T
    grad_wup = share(*pieces(norm_low2, pre_grad, 4))
    grad_wout = share(*pieces(proj_grad, mixture, 4)).T

    back = pl.pallas_call(
        qkv_back_kernel,
        name="qkv_back",
        in_specs=[smem()] + [vmem()] * (blocks + 4),
        out_specs=[vmem()] * 5,
        out_shape=[shaped((tokens, 3 * LANES), bf16)] * 4 + [shaped((tokens, width), bf16)],
        scratch_shapes=[pltpu.VMEM((blocks, images, pack_rows, LANES), bf16)],
    )(z_arg, *pack_grads, *wqkv)
    qkv_grads, norm1_part = back[:4], back[4]
    grad_wqkv = share(*[mm(norm_low1, g, TN).astype(bf16) for g in qkv_grads])
    grad_wqkv = grad_wqkv.reshape(piece_rows, 2, 3, middle).transpose(0, 2, 1, 3)
    grad_wqkv = grad_wqkv.reshape(piece_rows, 3, columns)

    norm1_grad = add(norm1_part, partner(norm1_part))
    _, normed1, inv_std1 = layer_norm(residual_in, gain1, shift1)
    grad_gain1 = jnp.sum(norm1_grad * normed1, axis=0)
    grad_shift1 = jnp.sum(norm1_grad, axis=0)
    input_grad = middle_grad + norm_back(norm1_grad * gain1, normed1, inv_std1)

    summed = jnp.stack([jnp.sum(g.astype(f32), axis=0) for g in qkv_grads])
    summed = summed.reshape(2, 2, 3, 2 * HD)[:, :, jnp.array([0, 2])].transpose(0, 2, 1, 3)
    qv_grad = summed.reshape(2, 2, b_qv.shape[1], shards, n_qv_last)
    qv_grad = qv_grad.transpose(0, 3, 1, 2, 4).reshape(2, shards, n_qv)
    up_grad = grad_bup.reshape(2, b_up.shape[0], shards, n_up_last)
    up_grad = up_grad.transpose(0, 2, 1, 3).reshape(2, shards, n_up)
    biases = jnp.take(jnp.concatenate([qv_grad, up_grad], axis=2), actual_of, axis=1)
    dense = jnp.stack(
        [
            grad_bout,
            grad_bdown,
            grad_gain1,
            grad_shift1,
            grad_gain2,
            grad_shift2,
            grad_scale1,
            grad_scale2,
        ]
    )
    dense = dense.reshape(-1, shards, piece_rows).transpose(1, 0, 2).reshape(shards, n_vec)
    pad = jnp.zeros((shards, small_size - n_vec - n_qv - n_up), f32)
    own = jnp.concatenate([dense, biases[0], pad], axis=1).reshape(-1, LANES)
    other = jnp.concatenate([dense, biases[1], pad], axis=1).reshape(-1, LANES)
    total = over_context(over_shard(own + across(other))).reshape(-1)
    vec = total[:n_vec].reshape(-1, piece_rows)

    return (
        whole_rows(result),
        whole_rows(input_grad),
        grad_wqkv,
        total[n_vec : n_vec + n_qv].reshape(b_qv.shape),
        grad_wout,
        vec[0],
        grad_wup,
        total[n_vec + n_qv : n_vec + n_qv + n_up].reshape(b_up.shape),
        grad_wdown,
        vec[1],
        vec[2],
        vec[3],
        vec[4],
        vec[5],
        vec[6],
        vec[7],
    )


def solution(mesh):
    in_specs = (
        P("shard", "context", None),
        P("shard"),
        P(("shard", "context"), None, "tensor"),
        P(None, "tensor", ("shard", "context")),
        P("tensor", ("shard", "context")),
        P(("shard", "context")),
        P(("shard", "context"), "tensor"),
        P("tensor", ("shard", "context")),
        P("tensor", ("shard", "context")),
        P(("shard", "context")),
        P(("shard", "context")),
        P(("shard", "context")),
        P(("shard", "context")),
        P(("shard", "context")),
        P(("shard", "context")),
        P(("shard", "context")),
        P("shard", "context", None),
    )
    out_specs = (
        P("shard", "context", None),
        P("shard", "context", None),
        P(("shard", "context"), None, "tensor"),
        P(None, "tensor", ("shard", "context")),
        P("tensor", ("shard", "context")),
        P(("shard", "context")),
        P(("shard", "context"), "tensor"),
        P("tensor", ("shard", "context")),
        P("tensor", ("shard", "context")),
        P(("shard", "context")),
        P(("shard", "context")),
        P(("shard", "context")),
        P(("shard", "context")),
        P(("shard", "context")),
        P(("shard", "context")),
        P(("shard", "context")),
    )
    sizes = tuple(mesh.shape[name] for name in ("shard", "context", "tensor"))
    return jax.shard_map(
        functools.partial(per_device, sizes),
        mesh=mesh,
        in_specs=in_specs,
        out_specs=out_specs,
        check_vma=False,
    )
```

```python
import functools

import jax
import jax.numpy as jnp
from jax import lax
from jax.experimental import pallas as pl
from jax.experimental.pallas import tpu as pltpu
from jax.sharding import Mesh
from jax.sharding import PartitionSpec as P

HD = 64
LANES = 128
CORES = 2
SMALL_ROWS = 16
SMALL_LANES = 3 * LANES

eps_norm = 1e-06
masked_score = -1e30
root_half = 0.7071067811865476
inv_root_two_pi = 0.3989422804014327
score_scale = HD ** (-0.5)

bf16 = jnp.bfloat16
f32 = jnp.float32
NN = (((1,), (0,)), ((), ()))
NT = (((1,), (1,)), ((), ()))

B_OUT, B_DOWN, GAIN1, SHIFT1, GAIN2, SHIFT2, SCALE1, SCALE2 = range(8)


def mm(left, right, dims=NN):
    return lax.dot_general(left, right, dims, preferred_element_type=f32)


def turn(values):
    return jnp.transpose(values.astype(f32)).astype(bf16)


def normalise(values):
    average = jnp.mean(values, axis=-1, keepdims=True)
    centred = values - average
    variance = jnp.mean(centred * centred, axis=-1, keepdims=True)
    inv_std = lax.rsqrt(variance + eps_norm)
    return centred * inv_std, inv_std


def norm_back(grad_in, normed, inv_std):
    first_mean = jnp.mean(grad_in, axis=-1, keepdims=True)
    second_mean = jnp.mean(grad_in * normed, axis=-1, keepdims=True)
    return inv_std * (grad_in - first_mean - normed * second_mean)


def row(table, index):
    return table[index : index + 1, :]


def column_sum(values):
    return jnp.sum(values, axis=0, keepdims=True)


def low_lanes(shape):
    return lax.broadcasted_iota(jnp.int32, shape, 1) < HD


def swap(values):
    return pltpu.roll(values, HD, 1)


def fold(wide):
    half = wide.shape[0] // 2
    return wide[:half] + swap(wide[half:])


def unfold(folded):
    low = low_lanes(folded.shape)
    return jnp.concatenate(
        [jnp.where(low, folded, 0.0), jnp.where(low, swap(folded), 0.0)], axis=0
    )


def owner_of(place_ref, slot, context):
    z, y = place_ref[1], place_ref[2]
    group = y if slot < context else 1 - y
    return group * context + lax.rem(z + slot % context, context)


def spread_mask(sc, last, columns):
    entry = lax.broadcasted_iota(jnp.int32, (LANES, columns), 0)
    column = lax.broadcasted_iota(jnp.int32, (LANES, columns), 1)
    return jnp.where(
        (entry < last) & (lax.rem(column, HD) == sc * last + entry), 1.0, 0.0
    ).astype(bf16)


def stack_kernel(place_ref, *refs):
    count = (len(refs) - 3) // 2
    pieces, smalls = refs[:count], refs[count : 2 * count]
    top_ref, bottom_ref, whole = refs[2 * count :]
    z = place_ref[1]
    rows = pieces[0].shape[0]
    split = top_ref.shape[0]
    whole[count * rows :, :] = jnp.zeros_like(whole[count * rows :, :])
    for j in range(count):
        spot = lax.rem(z - j + count, count)
        whole[pl.ds(pl.multiple_of(spot * rows, 16), rows), :] = pieces[j][...]
        start = pl.multiple_of(count * rows + spot * SMALL_ROWS, 16)
        whole[pl.ds(start, SMALL_ROWS), :SMALL_LANES] = smalls[j][...]
    top_ref[...] = whole[:split]
    bottom_ref[...] = whole[split:]


def qkv_kernel(sizes, place_ref, x_ref, *refs):
    n_shard, n_context, images, last, blocks = sizes
    n_stack = 4 * n_shard
    stacks, outs = refs[:n_stack], refs[n_stack : n_stack + blocks]
    norm_ref, wqkv_ref, wout_ref, vec_ref, bup_ref = refs[n_stack + blocks : n_stack + blocks + 5]
    scratch, bias_ref = refs[n_stack + blocks + 5 :]
    x, y = place_ref[0], place_ref[2]
    width = x_ref.shape[1]
    part_rows = width // n_shard
    piece_rows = part_rows // n_context
    head_columns = wout_ref.shape[2]
    qkv_columns = wqkv_ref.shape[2]
    up_columns = bup_ref.shape[2]
    vec = None
    for yr in range(2):
        y_spot = y if yr == 0 else 1 - y
        up, qv = None, None
        for xr in range(n_shard):
            x_spot = lax.rem(x - xr + n_shard, n_shard)
            top, bottom = stacks[4 * xr + 2 * yr], stacks[4 * xr + 2 * yr + 1]
            split = top.shape[0]
            start = pl.multiple_of(x_spot * part_rows, 16)
            here = pl.ds(start, split)
            wqkv_ref[y_spot, here, :] = top[:, :qkv_columns]
            wout_ref[y_spot, here, :] = top[:, qkv_columns:]
            rest = part_rows - split
            there = pl.ds(start + split, rest)
            wqkv_ref[y_spot, there, :] = bottom[:rest, :qkv_columns]
            wout_ref[y_spot, there, :] = bottom[:rest, qkv_columns:]
            for c in range(n_context):
                sc = x_spot * n_context + c
                lines = slice(rest + c * SMALL_ROWS, rest + (c + 1) * SMALL_ROWS)
                if yr == 0:
                    entry = lax.broadcasted_iota(jnp.int32, (LANES, width), 0)
                    column = lax.broadcasted_iota(jnp.int32, (LANES, width), 1)
                    place = jnp.where(
                        (entry < piece_rows) & (column == sc * piece_rows + entry), 1.0, 0.0
                    ).astype(bf16)
                    term = mm(bottom[lines, :LANES], place)
                    vec = term if vec is None else vec + term
                term = mm(bottom[lines, LANES : 2 * LANES], spread_mask(sc, last, up_columns))
                up = term if up is None else up + term
                term = mm(bottom[lines, 2 * LANES : 3 * LANES], spread_mask(sc, last, head_columns))
                qv = term if qv is None else qv + term
        line = lax.broadcasted_iota(jnp.int32, up.shape, 0)
        column = lax.broadcasted_iota(jnp.int32, up.shape, 1)
        bup_ref[y_spot] = column_sum(jnp.where(column // HD == line, up, 0.0))
        heads = head_columns // HD
        line = lax.broadcasted_iota(jnp.int32, qv.shape, 0)
        column = lax.broadcasted_iota(jnp.int32, qv.shape, 1) // HD
        bias_ref[y_spot, 0:1, :] = column_sum(jnp.where(column == line, qv, 0.0))
        bias_ref[y_spot, 1:2, :] = column_sum(jnp.where(column + heads == line, qv, 0.0))
    vec_ref[...] = vec
    rows = x_ref.shape[0] // images
    half = rows // 2
    normed, _ = normalise(x_ref[...].astype(f32))
    norm_low = (normed * row(vec, GAIN1) + row(vec, SHIFT1)).astype(bf16)
    norm_ref[...] = norm_low
    low = low_lanes((rows, LANES))
    low_half = low_lanes((half, LANES))
    for group in range(2):
        block = mm(norm_low, wqkv_ref[group])
        queries = block[:, :head_columns] + bias_ref[group, 0:1, :]
        keys = block[:, head_columns : 2 * head_columns]
        values = block[:, 2 * head_columns :] + bias_ref[group, 1:2, :]
        for pair in range(head_columns // LANES):
            lanes = slice(pair * LANES, (pair + 1) * LANES)
            head = group * n_context + 2 * pair
            for image in range(images):
                lines = slice(image * rows, (image + 1) * rows)
                query, key, value = queries[lines, lanes], keys[lines, lanes], values[lines, lanes]
                scratch[head, image, :rows] = jnp.where(low, query, swap(key)).astype(bf16)
                scratch[head + 1, image, :rows] = jnp.where(low, swap(query), key).astype(bf16)
                scratch[head, image, rows:] = jnp.where(
                    low_half, value[:half], swap(value[half:])
                ).astype(bf16)
                scratch[head + 1, image, rows:] = jnp.where(
                    low_half, swap(value[:half]), value[half:]
                ).astype(bf16)
    for slot in range(blocks):
        outs[slot][...] = scratch[owner_of(place_ref, slot, n_context)]


def attend_kernel(count_ref, pos_ref, *refs):
    blocks = (len(refs) - 3) // 2
    packs, outs, log_ref, keys, values = (
        refs[:blocks],
        refs[blocks : 2 * blocks],
        refs[2 * blocks],
        refs[2 * blocks + 1],
        refs[2 * blocks + 2],
    )
    rows = packs[0].shape[1] * 2 // 3
    low = low_lanes((rows, LANES))
    for j in range(blocks):
        pack = packs[j][0].astype(f32)
        keys[j * rows : (j + 1) * rows] = jnp.where(low, swap(pack[:rows]), 0.0).astype(bf16)
        values[j * rows : (j + 1) * rows] = unfold(pack[rows:]).astype(bf16)
    valid = pos_ref[...] < count_ref[pl.program_id(0)]
    for j in range(blocks):
        query = packs[j][0, :rows] * bf16(score_scale)
        scores = jnp.where(valid, mm(query, keys[...], NT), masked_score)
        highest = jnp.max(scores, axis=1, keepdims=True)
        exponent = jnp.exp(scores - highest)
        total = jnp.sum(exponent, axis=1, keepdims=True)
        mixed = mm(exponent.astype(bf16), values[...]) / total
        outs[j][0] = fold(mixed).astype(bf16)
        log_ref[0, j * rows : (j + 1) * rows] = highest + jnp.log(total)


def attend_back_kernel(count_ref, pos_ref, log_ref, *refs):
    blocks = (len(refs) - 4) // 4
    packs, mixes, grads, outs = (refs[i * blocks : (i + 1) * blocks] for i in range(4))
    keys, values, sums, query_grads = refs[4 * blocks :]
    rows = packs[0].shape[1] * 2 // 3
    half = rows // 2
    low = low_lanes((rows, LANES))
    low_half = low_lanes((half, LANES))
    for j in range(blocks):
        pack = packs[j][0].astype(f32)
        keys[j * rows : (j + 1) * rows] = jnp.where(low, swap(pack[:rows]), 0.0).astype(bf16)
        values[j * rows : (j + 1) * rows] = unfold(pack[rows:]).astype(bf16)
    valid = pos_ref[...] < count_ref[pl.program_id(0)]
    for j in range(blocks):
        query = packs[j][0, :rows] * bf16(score_scale)
        grad_wide = unfold(grads[j][0].astype(f32))
        mix_wide = unfold(mixes[j][0].astype(f32))
        delta = jnp.sum(grad_wide * mix_wide, axis=1, keepdims=True)
        grad = grad_wide.astype(bf16)
        scores = jnp.where(valid, mm(query, keys[...], NT), masked_score)
        probs = jnp.exp(scores - log_ref[0, j * rows : (j + 1) * rows])
        weight_grad = mm(grad, values[...], NT)
        score_grad = (probs * (weight_grad - delta)).astype(bf16)
        query_grads[j] = mm(score_grad, keys[...]) * score_scale
        query_t = jnp.transpose(query.astype(f32))[:HD].astype(bf16)
        grad_t = jnp.transpose(grad_wide)[:HD].astype(bf16)
        key_part = mm(query_t, score_grad)
        value_part = mm(grad_t, probs.astype(bf16))
        if j == 0:
            sums[:HD] = key_part
            sums[HD:] = value_part
        else:
            sums[:HD] = sums[:HD] + key_part
            sums[HD:] = sums[HD:] + value_part
    for j in range(blocks):
        both = jnp.transpose(sums[:, j * rows : (j + 1) * rows])
        outs[j][0, :rows] = jnp.where(low, query_grads[j], swap(both)).astype(bf16)
        outs[j][0, rows:] = jnp.where(low_half, swap(both[:half]), both[half:]).astype(bf16)


def project_kernel(n_context, place_ref, *refs):
    blocks = len(refs) - 4
    folded, (weight_ref, mixed_ref, part_ref, scratch) = refs[:blocks], refs[blocks:]
    images, half, _ = folded[0].shape
    rows = 2 * half
    for slot in range(blocks):
        scratch[owner_of(place_ref, slot, n_context)] = folded[slot][...]
    low = low_lanes((half, LANES))
    for pair in range(blocks // 2):
        columns = slice(pair * LANES, (pair + 1) * LANES)
        for image in range(images):
            first = scratch[2 * pair, image].astype(f32)
            second = scratch[2 * pair + 1, image].astype(f32)
            start = image * rows
            mixed_ref[start : start + half, columns] = jnp.where(
                low, first, swap(second)
            ).astype(bf16)
            mixed_ref[start + half : start + rows, columns] = jnp.where(
                low, swap(first), second
            ).astype(bf16)
    size = weight_ref.shape[2]
    part_ref[...] = (
        mm(mixed_ref[:, :size], weight_ref[0], NT) + mm(mixed_ref[:, size:], weight_ref[1], NT)
    ).astype(bf16)


def mlp_kernel(
    x_ref, cot_ref, part_ref, other_ref, vec_ref, bup_ref, feed_ref,
    norm_ref, grad_ref, act_ref, pre_ref, parts_ref, gup_ref,
):
    tokens = x_ref.shape[0]
    vec = vec_ref[...]
    branch = part_ref[...].astype(f32) + other_ref[...].astype(f32) + row(vec, B_OUT)
    middle = x_ref[...].astype(f32) + row(vec, SCALE1) * branch
    normed, _ = normalise(middle)
    norm_low = (normed * row(vec, GAIN2) + row(vec, SHIFT2)).astype(bf16)
    norm_ref[...] = norm_low
    branch_grad = (row(vec, SCALE2) * cot_ref[...].astype(f32)).astype(bf16)
    grad_ref[...] = branch_grad
    width = x_ref.shape[1]
    per_group = feed_ref.shape[1] // 2
    step = per_group // 2
    down, back = None, None
    for group in range(2):
        lines = slice(group * width, (group + 1) * width)
        for part in range(2):
            columns = slice(part * step, (part + 1) * step)
            up = feed_ref[lines, columns]
            turned = feed_ref[lines, per_group + part * step : per_group + (part + 1) * step]
            target = slice(group * per_group + part * step, group * per_group + (part + 1) * step)
            pre = mm(norm_low, up) + bup_ref[group, :, columns]
            erf_term = 0.5 * (1.0 + lax.erf(pre * root_half))
            act = (pre * erf_term).astype(bf16)
            act_ref[:, target] = act
            term = mm(act, turned, NT)
            down = term if down is None else down + term
            slope = erf_term + pre * inv_root_two_pi * jnp.exp(-0.5 * pre * pre)
            pre_grad = (mm(branch_grad, turned) * slope).astype(bf16)
            pre_ref[:, target] = pre_grad
            gup_ref[:, target] = column_sum(pre_grad.astype(f32))
            term = mm(pre_grad, up, NT)
            back = term if back is None else back + term
    parts_ref[:tokens] = down.astype(bf16)
    parts_ref[tokens:] = back.astype(bf16)


def mlp_weights_kernel(norm_ref, grad_ref, act_ref, pre_ref, out_ref):
    width = norm_ref.shape[1]
    per_group = act_ref.shape[1] // 2
    norm_t, grad_t = turn(norm_ref[...]), turn(grad_ref[...])
    for group in range(2):
        columns = slice(group * per_group, (group + 1) * per_group)
        lines = slice(group * width, (group + 1) * width)
        out_ref[lines, :per_group] = mm(norm_t, pre_ref[:, columns]).astype(bf16)
        out_ref[lines, per_group:] = mm(grad_t, act_ref[:, columns]).astype(bf16)


def back_kernel(
    images, n_context, place_ref, x_ref, cot_ref, part_ref, other_ref, parts_ref, others_ref,
    vec_ref, weight_ref, *refs
):
    result_ref, middle_grad_ref, proj_ref, sums_ref = refs[:4]
    outs, scratch = refs[4:-1], refs[-1]
    tokens = x_ref.shape[0]
    vec = vec_ref[...]
    upstream = cot_ref[...].astype(f32)
    branch = part_ref[...].astype(f32) + other_ref[...].astype(f32) + row(vec, B_OUT)
    middle = x_ref[...].astype(f32) + row(vec, SCALE1) * branch
    normed, inv_std = normalise(middle)
    mlp = parts_ref[:tokens].astype(f32) + others_ref[:tokens].astype(f32) + row(vec, B_DOWN)
    result_ref[...] = (middle + row(vec, SCALE2) * mlp).astype(bf16)
    norm_grad = parts_ref[tokens:].astype(f32) + others_ref[tokens:].astype(f32)
    middle_grad = upstream + norm_back(norm_grad * row(vec, GAIN2), normed, inv_std)
    middle_grad_ref[...] = middle_grad
    proj_wide = row(vec, SCALE1) * middle_grad
    proj = proj_wide.astype(bf16)
    proj_ref[...] = proj
    sums_ref[...] = jnp.zeros_like(sums_ref)
    for place, value in (
        (B_OUT, proj_wide),
        (B_DOWN, row(vec, SCALE2) * upstream),
        (GAIN2, norm_grad * normed),
        (SHIFT2, norm_grad),
        (SCALE1, middle_grad * branch),
        (SCALE2, upstream * mlp),
    ):
        sums_ref[place : place + 1, :] = column_sum(value)
    rows = tokens // images
    half = rows // 2
    low = low_lanes((half, LANES))
    size = weight_ref.shape[2]
    for group in range(2):
        wide = mm(proj, weight_ref[group])
        for pair in range(size // LANES):
            head = group * n_context + 2 * pair
            for image in range(images):
                block = wide[image * rows : (image + 1) * rows, pair * LANES : (pair + 1) * LANES]
                first, second = block[:half], block[half:]
                scratch[head, image] = jnp.where(low, first, swap(second)).astype(bf16)
                scratch[head + 1, image] = jnp.where(low, swap(first), second).astype(bf16)
    for slot in range(len(outs)):
        outs[slot][...] = scratch[owner_of(place_ref, slot, n_context)]


def qkv_back_kernel(sizes, place_ref, *refs):
    n_shard, n_context, blocks = sizes
    packs = refs[:blocks]
    weight_ref, norm_ref, proj_ref, mixed_ref = refs[blocks : blocks + 4]
    part_ref, sum_ref = refs[blocks + 4 : blocks + 6]
    quads = refs[blocks + 6 : -2]
    scratch, grads = refs[-2:]
    images = packs[0].shape[0]
    rows = packs[0].shape[1] * 2 // 3
    half = rows // 2
    columns = mixed_ref.shape[1] // 2
    for slot in range(blocks):
        scratch[owner_of(place_ref, slot, n_context)] = packs[slot][...]
    low = low_lanes((rows, LANES))
    low_half = low_lanes((half, LANES))
    total = None
    for group in range(2):
        for pair in range(columns // LANES):
            head = group * n_context + 2 * pair
            lanes = slice(pair * LANES, (pair + 1) * LANES)
            for image in range(images):
                first = scratch[head, image].astype(f32)
                second = scratch[head + 1, image].astype(f32)
                start = image * rows
                here = slice(start, start + rows)
                grads[group, 0, here, lanes] = jnp.where(
                    low, first[:rows], swap(second[:rows])
                ).astype(bf16)
                grads[group, 1, here, lanes] = jnp.where(
                    low, swap(first[:rows]), second[:rows]
                ).astype(bf16)
                grads[group, 2, start : start + half, lanes] = jnp.where(
                    low_half, first[rows:], swap(second[rows:])
                ).astype(bf16)
                grads[group, 2, start + half : start + rows, lanes] = jnp.where(
                    low_half, swap(first[rows:]), second[rows:]
                ).astype(bf16)
        for part in range(3):
            term = mm(
                grads[group, part],
                weight_ref[group, :, part * columns : (part + 1) * columns],
                NT,
            )
            total = term if total is None else total + term
        sum_ref[group, 0:1, :] = column_sum(grads[group, 0].astype(f32))
        sum_ref[group, 1:2, :] = column_sum(grads[group, 2].astype(f32))
    part_ref[...] = total.astype(bf16)
    x, y = place_ref[0], place_ref[2]
    part_rows = norm_ref.shape[1] // n_shard
    split = part_rows // 2
    for xr in range(n_shard):
        x_spot = lax.rem(x - xr + n_shard, n_shard)
        lanes = pl.ds(pl.multiple_of(x_spot * part_rows, LANES), part_rows)
        norm_part, proj_part = turn(norm_ref[:, lanes]), turn(proj_ref[:, lanes])
        for yr in range(2):
            y_spot = y if yr == 0 else 1 - y
            top, bottom = quads[4 * xr + 2 * yr], quads[4 * xr + 2 * yr + 1]
            mixed = mixed_ref[:, pl.ds(pl.multiple_of(y_spot * columns, LANES), columns)]
            for part in range(4):
                if part < 3:
                    value = mm(norm_part, grads[y_spot, part])
                else:
                    value = mm(proj_part, mixed)
                place = slice(part * columns, (part + 1) * columns)
                top[:, place] = value[:split].astype(bf16)
                bottom[:, place] = value[split:].astype(bf16)


def finish_kernel(
    sizes, place_ref, x_ref, middle_grad_ref, part_ref, other_ref, vec_ref, sums_ref, gup_ref,
    gqv_ref, out_ref, own_ref, far_ref,
):
    n_shard, n_context, last = sizes
    x, z, y = place_ref[0], place_ref[1], place_ref[2]
    width = x_ref.shape[1]
    piece_rows = width // (n_shard * n_context)
    norm_grad = part_ref[...].astype(f32) + other_ref[...].astype(f32)
    normed, inv_std = normalise(x_ref[...].astype(f32))
    gain = vec_ref[GAIN1 : GAIN1 + 1, :]
    out_ref[...] = (
        middle_grad_ref[...] + norm_back(norm_grad * gain, normed, inv_std)
    ).astype(bf16)
    line = lax.broadcasted_iota(jnp.int32, sums_ref.shape, 0)
    sums = jnp.where(line == GAIN1, column_sum(norm_grad * normed), sums_ref[...])
    sums = jnp.where(line == SHIFT1, column_sum(norm_grad), sums).astype(bf16)
    heads = gqv_ref.shape[2] // HD
    for target, y_spot in ((own_ref, y), (far_ref, 1 - y)):
        up = gup_ref[y_spot]
        line = lax.broadcasted_iota(jnp.int32, (SMALL_ROWS, up.shape[1]), 0)
        column = lax.broadcasted_iota(jnp.int32, (SMALL_ROWS, up.shape[1]), 1) // HD
        up = jnp.where(column == line, up, 0.0).astype(bf16)
        both = gqv_ref[y_spot]
        line = lax.broadcasted_iota(jnp.int32, (SMALL_ROWS, both.shape[1]), 0)
        column = lax.broadcasted_iota(jnp.int32, (SMALL_ROWS, both.shape[1]), 1) // HD
        qv = jnp.where(column == line, both[0:1], 0.0)
        qv = (qv + jnp.where(column + heads == line, both[1:2], 0.0)).astype(bf16)
        for xr in range(n_shard):
            for zr in range(n_context):
                sc = lax.rem(x - xr + n_shard, n_shard) * n_context
                sc = sc + lax.rem(z - zr + n_context, n_context)
                start = (xr * n_context + zr) * SMALL_ROWS
                lines = slice(start, start + SMALL_ROWS)
                entry = lax.broadcasted_iota(jnp.int32, (LANES, width), 0)
                column = lax.broadcasted_iota(jnp.int32, (LANES, width), 1)
                place = jnp.where(
                    (entry < piece_rows) & (column == sc * piece_rows + entry), 1.0, 0.0
                ).astype(bf16)
                target[lines, :LANES] = mm(sums, place, NT)
                target[lines, LANES : 2 * LANES] = mm(
                    up, spread_mask(sc, last, up.shape[1]), NT
                )
                target[lines, 2 * LANES :] = mm(qv, spread_mask(sc, last, qv.shape[1]), NT)


def deal_kernel(place_ref, *refs):
    own_top, own_bottom = refs[0], refs[1]
    tops, bottoms, outs, whole = refs[2], refs[3], refs[4], refs[5]
    z = place_ref[1]
    split = own_top.shape[0]
    count = len(outs)
    top, bottom = own_top[...].astype(f32), own_bottom[...].astype(f32)
    for ref in tops:
        top = top + ref[...].astype(f32)
    for ref in bottoms:
        bottom = bottom + ref[...].astype(f32)
    whole[:split] = top
    whole[split:] = bottom
    rows = 2 * split // count
    for j in range(count):
        spot = lax.rem(z - j + count, count)
        value = whole[pl.ds(pl.multiple_of(spot * rows, 16), rows), :]
        outs[j][...] = value.astype(outs[j].dtype)


def merge_kernel(place_ref, own_ref, near_ref, far_ref, out_ref):
    y, core = place_ref[2], place_ref[3]
    images, _, width = out_ref.shape
    tokens = own_ref.shape[0]
    rows = tokens // images
    half = tokens // 2
    other = lambda first: jnp.where(core == first, near_ref[...], far_ref[...])
    first, second = other(0).astype(f32), other(1).astype(f32)
    both = jnp.concatenate([first, second], axis=0)
    for image in range(images):
        lines = slice(image * rows, (image + 1) * rows)
        here = pl.ds(pl.multiple_of(y * rows, 8), rows)
        there = pl.ds(pl.multiple_of((1 - y) * rows, 8), rows)
        out_ref[image, here, :] = own_ref[lines, :].astype(f32)
        out_ref[image, there, :] = both[lines]


def vmem():
    return pl.BlockSpec(memory_space=pltpu.VMEM)


def smem():
    return pl.BlockSpec(memory_space=pltpu.SMEM)


def shaped(shape, dtype):
    return jax.ShapeDtypeStruct(shape, dtype)


def call(kernel, name, out_shape, scratch, place, *operands):
    return pl.pallas_call(
        kernel,
        name=name,
        in_specs=[smem()] + [vmem()] * len(operands),
        out_specs=[vmem()] * len(out_shape),
        out_shape=out_shape,
        scratch_shapes=scratch,
    )(place, *operands)


def per_device(sizes, *args):
    (
        tokens_in,
        counts,
        w_qkv,
        b_qv,
        w_out,
        b_out,
        w_up,
        b_up,
        w_down,
        b_down,
        norm1_gain,
        norm1_bias,
        norm2_gain,
        norm2_bias,
        scale1,
        scale2,
        cotangent,
    ) = args
    n_shard, n_context, n_y = sizes
    images, row_count, width = tokens_in.shape
    piece_rows = w_qkv.shape[0]
    head_columns = w_qkv.shape[2]
    hidden = w_up.shape[1]
    last = b_up.shape[1]
    rows = row_count // n_y
    half = rows // 2
    tokens = images * rows
    x = lax.axis_index("shard")
    z = lax.axis_index("context")
    y = lax.axis_index("y")
    core = lax.axis_index("core")
    place = jnp.stack([x, z, y, core]).astype(jnp.int32)
    blocks = n_y * n_context
    everyone = ("y", "shard", "context")

    def send(value, axis, step):
        size = {"shard": n_shard, "context": n_context}[axis]
        return lax.ppermute(value, axis, [(i, (i + step) % size) for i in range(size)])

    def across(value):
        return lax.ppermute(value, "y", [(0, 1), (1, 0)])

    def partner(value):
        return lax.ppermute(value, "core", [(0, 1), (1, 0)])

    def hand_over(values, back):
        out = [values[0]]
        for slot in range(1, blocks):
            jy, jz = slot // n_context, slot % n_context
            step = -jz if back else jz
            pairs = [
                (i * n_y + t, (i + step) % n_context * n_y + (t ^ jy))
                for i in range(n_context)
                for t in range(n_y)
            ]
            out.append(lax.ppermute(values[slot], ("context", "y"), pairs))
        return out

    feed = lax.all_gather(
        jnp.concatenate([w_up, w_down.T], axis=1), everyone, axis=0, tiled=True
    )

    piece = jnp.concatenate([w_qkv.reshape(piece_rows, -1), w_out.T], axis=1)
    vectors = [b_out, b_down, norm1_gain, norm1_bias, norm2_gain, norm2_bias, scale1, scale2]

    def block_of(value):
        return jnp.pad(value, ((0, SMALL_ROWS - value.shape[0]), (0, LANES - value.shape[1])))

    small = jnp.concatenate(
        [block_of(jnp.stack(vectors)), block_of(b_up), block_of(b_qv.reshape(-1, last))], axis=1
    )
    pieces = [piece] + [send(piece, "context", j) for j in range(1, n_context)]
    smalls = [small] + [send(small, "context", j) for j in range(1, n_context)]
    stack_rows = n_context * (piece_rows + SMALL_ROWS)
    split = stack_rows // 2
    columns = piece.shape[1]
    top, bottom = call(
        stack_kernel,
        "stack",
        [shaped((split, columns), bf16)] * 2,
        [pltpu.VMEM((stack_rows, columns), bf16)],
        place,
        *pieces,
        *smalls,
    )
    y_bottom = across(bottom)
    x_tops = [send(top, "shard", j) for j in range(1, n_shard)]
    x_bottoms = [send(bottom, "shard", j) for j in range(1, n_shard)]
    y_top = across(top)
    far_tops = [across(value) for value in x_tops]
    far_bottoms = [send(y_bottom, "shard", j) for j in range(1, n_shard)]
    stacks = [top, bottom, y_top, y_bottom]
    for j in range(n_shard - 1):
        stacks += [x_tops[j], x_bottoms[j], far_tops[j], far_bottoms[j]]

    def own_rows(array):
        return lax.dynamic_slice_in_dim(array, y * rows, rows, 1).reshape(tokens, width)

    residual = own_rows(tokens_in)
    upstream = own_rows(cotangent)

    pack_rows = rows + half
    packed = call(
        functools.partial(qkv_kernel, (n_shard, n_context, images, last, blocks)),
        "qkv",
        [shaped((images, pack_rows, LANES), bf16)] * blocks
        + [
            shaped((tokens, width), bf16),
            shaped((n_y, width, 3 * head_columns), bf16),
            shaped((n_y, width, head_columns), bf16),
            shaped((SMALL_ROWS, width), f32),
            shaped((n_y, 1, hidden), f32),
        ],
        [
            pltpu.VMEM((blocks, images, pack_rows, LANES), bf16),
            pltpu.VMEM((n_y, 8, head_columns), f32),
        ],
        place,
        residual,
        *stacks,
    )
    norm_low1, wqkv, wout, vec, bup = packed[blocks:]
    packs = hand_over(packed[:blocks], False)

    slot = jnp.arange(blocks)
    source = (z - slot % n_context) % n_context * row_count + (y ^ (slot // n_context)) * rows
    key_place = (source[:, None] + jnp.arange(rows)[None, :]).reshape(1, -1).astype(jnp.int32)
    length = blocks * rows
    pack_spec = pl.BlockSpec((1, pack_rows, LANES), lambda i: (i, 0, 0))
    fold_spec = pl.BlockSpec((1, half, LANES), lambda i: (i, 0, 0))
    pos_spec = pl.BlockSpec((1, length), lambda i: (0, 0))
    log_spec = pl.BlockSpec((1, length, 1), lambda i: (i, 0, 0))
    attended = pl.pallas_call(
        attend_kernel,
        name="attend",
        grid=(images,),
        in_specs=[smem(), pos_spec] + [pack_spec] * blocks,
        out_specs=[fold_spec] * blocks + [log_spec],
        out_shape=[shaped((images, half, LANES), bf16)] * blocks
        + [shaped((images, length, 1), f32)],
        scratch_shapes=[pltpu.VMEM((length, LANES), bf16)] * 2,
    )(counts, key_place, *packs)
    mixes, log_total = attended[:blocks], attended[blocks]
    folded = hand_over(mixes, True)

    fold_scratch = pltpu.VMEM((blocks, images, half, LANES), bf16)
    mixture, proj_part = call(
        functools.partial(project_kernel, n_context),
        "project",
        [shaped((tokens, blocks * HD), bf16), shaped((tokens, width), bf16)],
        [fold_scratch],
        place,
        *folded,
        wout,
    )
    proj_other = partner(proj_part)

    norm_low2, branch_grad, hidden_act, pre_grad, parts, grad_bup = pl.pallas_call(
        mlp_kernel,
        name="mlp",
        in_specs=[vmem()] * 7,
        out_specs=[vmem()] * 6,
        out_shape=[
            shaped((tokens, width), bf16),
            shaped((tokens, width), bf16),
            shaped((tokens, n_y * hidden), bf16),
            shaped((tokens, n_y * hidden), bf16),
            shaped((2 * tokens, width), bf16),
            shaped((1, n_y * hidden), f32),
        ],
    )(residual, upstream, proj_part, proj_other, vec, bup, feed)
    others = partner(parts)
    feed_grad = pl.pallas_call(
        mlp_weights_kernel,
        name="mlp_weights",
        in_specs=[vmem()] * 4,
        out_specs=vmem(),
        out_shape=shaped((n_y * width, 2 * hidden), bf16),
    )(norm_low2, branch_grad, hidden_act, pre_grad)
    feed_grad = lax.psum_scatter(feed_grad, everyone, scatter_dimension=0, tiled=True)

    back = call(
        functools.partial(back_kernel, images, n_context),
        "back",
        [
            shaped((tokens, width), bf16),
            shaped((tokens, width), f32),
            shaped((tokens, width), bf16),
            shaped((SMALL_ROWS, width), f32),
        ]
        + [shaped((images, half, LANES), bf16)] * blocks,
        [fold_scratch],
        place,
        residual,
        upstream,
        proj_part,
        proj_other,
        parts,
        others,
        vec,
        wout,
    )
    result, middle_grad, proj_grad, sums = back[:4]
    mix_grads = hand_over(back[4:], False)

    pack_grads = pl.pallas_call(
        attend_back_kernel,
        name="attend_back",
        grid=(images,),
        in_specs=[smem(), pos_spec, log_spec]
        + [pack_spec] * blocks
        + [fold_spec] * (2 * blocks),
        out_specs=[pack_spec] * blocks,
        out_shape=[shaped((images, pack_rows, LANES), bf16)] * blocks,
        scratch_shapes=[pltpu.VMEM((length, LANES), bf16)] * 2
        + [pltpu.VMEM((2 * HD, length), f32), pltpu.VMEM((blocks, rows, LANES), f32)],
    )(counts, key_place, log_total, *packs, *mixes, *mix_grads)
    pack_grads = hand_over(pack_grads, True)

    part_rows = n_context * piece_rows
    last_back = call(
        functools.partial(qkv_back_kernel, (n_shard, n_context, blocks)),
        "qkv_back",
        [shaped((tokens, width), bf16), shaped((n_y, 8, head_columns), f32)]
        + [shaped((part_rows // 2, columns), bf16)] * (4 * n_shard),
        [
            pltpu.VMEM((blocks, images, pack_rows, LANES), bf16),
            pltpu.VMEM((n_y, 3, tokens, head_columns), bf16),
        ],
        place,
        *pack_grads,
        wqkv,
        norm_low1,
        proj_grad,
        mixture,
    )
    norm1_part, grad_qv, quads = last_back[0], last_back[1], last_back[2:]

    def add(first, *rest):
        total = first.astype(f32)
        for value in rest:
            total = total + value.astype(f32)
        return total.astype(bf16)

    norm1_other = partner(norm1_part)
    tops, bottoms = [], []
    bottom_far = [quads[3]]
    for j in range(1, n_shard):
        x_top, x_bottom, far_top, far_bottom = quads[4 * j : 4 * j + 4]
        far_top = across(far_top)
        bottom_far.append(send(far_bottom, "shard", -j))
        bottoms.append(send(x_bottom, "shard", -j))
        tops.append(send(add(x_top, far_top), "shard", -j))
    tops.append(across(quads[2]))
    bottoms.append(across(add(*bottom_far)))
    dealt = pl.pallas_call(
        lambda place_ref, *refs: deal_kernel(
            place_ref,
            refs[0],
            refs[1],
            refs[2 : 2 + n_shard],
            refs[2 + n_shard : 2 + 2 * n_shard],
            refs[2 + 2 * n_shard : -1],
            refs[-1],
        ),
        name="deal",
        in_specs=[smem()] + [vmem()] * (2 + 2 * n_shard),
        out_specs=[vmem()] * n_context,
        out_shape=[shaped((piece_rows, columns), f32)]
        + [shaped((piece_rows, columns), bf16)] * (n_context - 1),
        scratch_shapes=[pltpu.VMEM((part_rows, columns), f32)],
    )(place, quads[0], quads[1], *tops, *bottoms)
    grad_piece = dealt[0]
    for j in range(1, n_context):
        grad_piece = grad_piece + send(dealt[j], "context", -j).astype(f32)

    input_grad, own, far = call(
        functools.partial(finish_kernel, (n_shard, n_context, last)),
        "finish",
        [shaped((tokens, width), bf16)]
        + [shaped((n_shard * n_context * SMALL_ROWS, SMALL_LANES), f32)] * 2,
        [],
        place,
        residual,
        middle_grad,
        norm1_part,
        norm1_other,
        vec,
        sums,
        grad_bup.reshape(n_y, 1, hidden),
        grad_qv,
    )
    total = (own + across(far)).reshape(n_shard, -1, SMALL_LANES)
    over_shard = total[0]
    for j in range(1, n_shard):
        over_shard = over_shard + send(total[j], "shard", -j)
    over_shard = over_shard.reshape(n_context, SMALL_ROWS, SMALL_LANES)
    small_grad = over_shard[0]
    for j in range(1, n_context):
        small_grad = small_grad + send(over_shard[j], "context", -j)

    def whole_rows(value):
        mine = lax.dynamic_slice_in_dim(value, core * (tokens // 2), tokens // 2, 0)
        near = across(mine)
        far = partner(near)
        return call(
            merge_kernel,
            "merge",
            [shaped((images, row_count, width), f32)],
            [],
            place,
            value,
            near,
            far,
        )[0]

    vec_grad = small_grad[: len(vectors), :piece_rows]
    return (
        whole_rows(result),
        whole_rows(input_grad),
        grad_piece[:, : 3 * head_columns].reshape(piece_rows, 3, head_columns),
        small_grad[: b_qv.shape[0] * b_qv.shape[1], 2 * LANES : 2 * LANES + last].reshape(
            b_qv.shape
        ),
        grad_piece[:, 3 * head_columns :].T,
        vec_grad[B_OUT],
        feed_grad[:, :hidden].astype(f32),
        small_grad[: b_up.shape[0], LANES : LANES + last],
        feed_grad[:, hidden:].astype(f32).T,
        vec_grad[B_DOWN],
        vec_grad[GAIN1],
        vec_grad[SHIFT1],
        vec_grad[GAIN2],
        vec_grad[SHIFT2],
        vec_grad[SCALE1],
        vec_grad[SCALE2],
    )


def solution(mesh):
    pair = ("y", "core")
    both = ("shard", "context")
    tokens = P("shard", "context", None)
    vector = P(both)
    in_specs = (
        tokens,
        P("shard"),
        P(both, None, pair),
        P(None, pair, both),
        P(pair, both),
        vector,
        P(both, pair),
        P(pair, both),
        P(pair, both),
    ) + (vector,) * 7
    in_specs = in_specs + (tokens,)
    out_specs = (
        tokens,
        tokens,
        P(both, None, pair),
        P(None, pair, both),
        P(pair, both),
        vector,
        P(both, pair),
        P(pair, both),
        P(pair, both),
    ) + (vector,) * 7
    sizes = tuple(mesh.shape[name] for name in ("shard", "context", "tensor"))
    split = Mesh(
        mesh.devices.reshape(sizes[0], sizes[1], sizes[2] // CORES, CORES),
        ("shard", "context", "y", "core"),
    )
    return jax.shard_map(
        functools.partial(per_device, split.devices.shape[:3]),
        mesh=split,
        in_specs=in_specs,
        out_specs=out_specs,
        check_vma=False,
    )
```

```python
import functools

import jax
import jax.numpy as jnp
from jax import lax
from jax.experimental import pallas as pl
from jax.experimental.pallas import tpu as pltpu
from jax.sharding import Mesh
from jax.sharding import PartitionSpec as P

HD = 64
LANES = 128
CORES = 2
SMALL_ROWS = 16
SMALL_LANES = 3 * LANES
FLOPS, BYTES = 1e+09, 3e+06

eps_norm = 1e-06
masked_score = -1e30
root_half = 0.7071067811865476
inv_root_two_pi = 0.3989422804014327
score_scale = HD ** (-0.5)

bf16 = jnp.bfloat16
f32 = jnp.float32
NN = (((1,), (0,)), ((), ()))
NT = (((1,), (1,)), ((), ()))

B_OUT, B_DOWN, GAIN1, SHIFT1, GAIN2, SHIFT2, SCALE1, SCALE2 = range(8)


def mm(left, right, dims=NN):
    return lax.dot_general(left, right, dims, preferred_element_type=f32)


def turn(values):
    return jnp.transpose(values.astype(f32)).astype(bf16)


def normalise(values):
    average = jnp.mean(values, axis=-1, keepdims=True)
    centred = values - average
    variance = jnp.mean(centred * centred, axis=-1, keepdims=True)
    inv_std = lax.rsqrt(variance + eps_norm)
    return centred * inv_std, inv_std


def norm_back(grad_in, normed, inv_std):
    first_mean = jnp.mean(grad_in, axis=-1, keepdims=True)
    second_mean = jnp.mean(grad_in * normed, axis=-1, keepdims=True)
    return inv_std * (grad_in - first_mean - normed * second_mean)


def row(table, index):
    return table[index : index + 1, :]


def column_sum(values):
    return jnp.sum(values, axis=0, keepdims=True)


def low_lanes(shape):
    return lax.broadcasted_iota(jnp.int32, shape, 1) < HD


def swap(values):
    return pltpu.roll(values, HD, 1)


def fold(wide):
    half = wide.shape[0] // 2
    return wide[:half] + swap(wide[half:])


def unfold(folded):
    low = low_lanes(folded.shape)
    return jnp.concatenate(
        [jnp.where(low, folded, 0.0), jnp.where(low, swap(folded), 0.0)], axis=0
    )


def owner_of(place_ref, slot, context):
    z, y = place_ref[1], place_ref[2]
    group = y if slot < context else 1 - y
    return group * context + lax.rem(z + slot % context, context)


def spread_mask(sc, last, columns):
    entry = lax.broadcasted_iota(jnp.int32, (LANES, columns), 0)
    column = lax.broadcasted_iota(jnp.int32, (LANES, columns), 1)
    return jnp.where(
        (entry < last) & (lax.rem(column, HD) == sc * last + entry), 1.0, 0.0
    ).astype(bf16)


def block_rows(step_rows):
    return -(-step_rows // (4 * SMALL_ROWS)) * SMALL_ROWS


def chunks_of(first, size, block):
    while size:
        count = min(size, block - first % block)
        yield first, count, first // block * 2 * LANES, first % block
        first, size = first + count, size - count


def bundle_kernel(place_ref, w_ref, small_ref, tokens_ref, own_ref, *refs):
    outs, scratch = refs[:-1], refs[-1]
    z, spot = place_ref[1], 2 * place_ref[2] + place_ref[3]
    rows = w_ref.shape[0]
    step_rows = rows + small_ref.shape[0]
    block = own_ref.shape[0]
    count = len(outs) + 1
    columns = w_ref.shape[1] // 3
    images, row_count, _ = tokens_ref.shape
    quarter = row_count // 4
    low = low_lanes((rows, LANES))
    scratch[...] = jnp.zeros_like(scratch)
    for head in range(count):
        first = head // 2 * LANES
        query, key, value = (
            w_ref[:, part * columns + first : part * columns + first + LANES].astype(f32)
            for part in range(3)
        )
        if head % 2:
            query, value = swap(query), swap(value)
        else:
            key = swap(key)
        both = jnp.where(low, query, key).astype(bf16)
        value = jnp.where(low, value, 0.0).astype(bf16)
        for start, size, lane, line in chunks_of(0, rows, block):
            here = slice(line, line + size)
            scratch[head, here, lane : lane + LANES] = both[start : start + size]
            scratch[head, here, lane + LANES : lane + 2 * LANES] = value[start : start + size]
        for start, size, lane, line in chunks_of(rows, step_rows - rows, block):
            here = slice(line, line + size)
            scratch[head, here, lane : lane + LANES] = small_ref[start - rows : start - rows + size]
    own_ref[...] = scratch[z]
    for j, out in enumerate(outs):
        for image in range(images):
            there = pl.ds(pl.multiple_of(spot * quarter, 16), quarter)
            out[image * quarter : (image + 1) * quarter, :] = tokens_ref[image, there, :]
        out[images * quarter :, :] = scratch[lax.rem(z + j + 1, count)]


def prepare_kernel(sizes, place_ref, *refs):
    n_shard, n_context, last, heads = sizes
    stacks = refs[:n_shard]
    weight_ref, vec_ref, bias_ref, bup_ref = refs[n_shard:]
    x, z = place_ref[0], place_ref[1]
    width = weight_ref.shape[0]
    piece_rows = width // (n_shard * n_context)
    block = stacks[0].shape[0] // n_context
    vec, qv, up = None, None, None
    for xr in range(n_shard):
        for zr in range(n_context):
            sc = lax.rem(x - xr + n_shard, n_shard) * n_context
            sc = sc + lax.rem(z - zr + n_context, n_context)
            stack = stacks[xr]
            base = pl.multiple_of(sc * piece_rows, 16)
            for start, size, lane, line in chunks_of(0, piece_rows, block):
                line = zr * block + line
                weight_ref[pl.ds(base + start, size), :] = stack[
                    line : line + size, lane : lane + 2 * LANES
                ]

            def small(index):
                start = piece_rows + index * SMALL_ROWS
                lane, line = start // block * 2 * LANES, zr * block + start % block
                return stack[line : line + SMALL_ROWS, lane : lane + LANES]

            entry = lax.broadcasted_iota(jnp.int32, (LANES, width), 0)
            column = lax.broadcasted_iota(jnp.int32, (LANES, width), 1)
            place = jnp.where(
                (entry < piece_rows) & (column == sc * piece_rows + entry), 1.0, 0.0
            ).astype(bf16)
            term = mm(small(0), place)
            vec = term if vec is None else vec + term
            term = mm(small(1), spread_mask(sc, last, bup_ref.shape[1]))
            up = term if up is None else up + term
            term = mm(small(2), spread_mask(sc, last, 2 * LANES))
            qv = term if qv is None else qv + term
    vec_ref[...] = vec
    line = lax.broadcasted_iota(jnp.int32, up.shape, 0)
    column = lax.broadcasted_iota(jnp.int32, up.shape, 1)
    bup_ref[...] = column_sum(jnp.where(column // HD == line, up, 0.0))
    line = lax.broadcasted_iota(jnp.int32, qv.shape, 0)
    column = lax.broadcasted_iota(jnp.int32, qv.shape, 1) // HD
    chosen = ((line == z) & (column == 0)) | ((line == heads + z) & (column == 2))
    bias_ref[...] = jnp.zeros_like(bias_ref)
    bias_ref[0:1, :] = column_sum(jnp.where(chosen, qv, 0.0))


def attend_kernel(
    n_context, count_ref, place_ref, pos_ref, weight_ref, vec_ref, bias_ref, own_ref, *refs
):
    blocks = 2 * n_context
    n_quarter = 4 * (n_context - 1)
    quarters = refs[:n_quarter]
    outs = refs[n_quarter : n_quarter + blocks]
    log_ref, norm_ref, qk_ref, v_ref, keys, tokens = refs[n_quarter + blocks :]
    y, core = place_ref[2], place_ref[3]
    rows = own_ref.shape[1] // 2
    half = rows // 2
    gain, shift = vec_ref[GAIN1 : GAIN1 + 1, :], vec_ref[SHIFT1 : SHIFT1 + 1, :]
    low = low_lanes((rows, LANES))
    for jz in range(n_context):
        for jy in range(2):
            slot = jy * n_context + jz
            lines = slice(slot * rows, (slot + 1) * rows)
            if jz == 0:
                first = pl.multiple_of((y if jy == 0 else 1 - y) * rows, 16)
                block = own_ref[0, pl.ds(first, rows), :]
            else:
                for other in range(2):
                    spot = core if other == 0 else 1 - core
                    first = pl.multiple_of(spot * half, 16)
                    quarter = quarters[4 * (jz - 1) + 2 * other + jy]
                    tokens[pl.ds(first, half), :] = quarter[...]
                block = tokens[...]
            normed, _ = normalise(block.astype(f32))
            norm_low = (normed * gain + shift).astype(bf16)
            norm_ref[0, lines, :] = norm_low
            qkv = mm(norm_low, weight_ref[...]) + bias_ref[0:1, :]
            qk_ref[0, lines, :] = qkv[:, :LANES].astype(bf16)
            v_ref[0, lines, :] = qkv[:, LANES:].astype(bf16)
            keys[lines, :] = jnp.where(low, swap(qkv[:, :LANES]), 0.0).astype(bf16)
    valid = pos_ref[...] < count_ref[pl.program_id(0)]
    for j in range(blocks):
        query = qk_ref[0, j * rows : (j + 1) * rows] * bf16(score_scale)
        scores = jnp.where(valid, mm(query, keys[...], NT), masked_score)
        highest = jnp.max(scores, axis=1, keepdims=True)
        exponent = jnp.exp(scores - highest)
        total = jnp.sum(exponent, axis=1, keepdims=True)
        mixed = mm(exponent.astype(bf16), v_ref[0]) / total
        outs[j][0] = fold(mixed).astype(bf16)
        log_ref[0, j * rows : (j + 1) * rows] = highest + jnp.log(total)


def attend_back_kernel(count_ref, pos_ref, log_ref, norm_ref, qk_ref, v_ref, *refs):
    blocks = (len(refs) - 6) // 3
    mixes, grads, outs = (refs[i * blocks : (i + 1) * blocks] for i in range(3))
    weight_ref, bias_ref, keys, sums, query_grads, turned = refs[3 * blocks :]
    rows = qk_ref.shape[1] // blocks
    half = rows // 2
    low = low_lanes((rows, LANES))
    low_half = low_lanes((half, LANES))
    for j in range(blocks):
        pack = qk_ref[0, j * rows : (j + 1) * rows].astype(f32)
        keys[j * rows : (j + 1) * rows] = jnp.where(low, swap(pack), 0.0).astype(bf16)
    valid = pos_ref[...] < count_ref[pl.program_id(0)]
    for j in range(blocks):
        lines = slice(j * rows, (j + 1) * rows)
        query = qk_ref[0, lines] * bf16(score_scale)
        grad_wide = unfold(grads[j][0].astype(f32))
        mix_wide = unfold(mixes[j][0].astype(f32))
        delta = jnp.sum(grad_wide * mix_wide, axis=1, keepdims=True)
        grad = grad_wide.astype(bf16)
        scores = jnp.where(valid, mm(query, keys[...], NT), masked_score)
        probs = jnp.exp(scores - log_ref[0, lines])
        weight_grad = mm(grad, v_ref[0], NT)
        score_grad = (probs * (weight_grad - delta)).astype(bf16)
        query_grads[lines] = mm(score_grad, keys[...]) * score_scale
        query_t = jnp.transpose(query.astype(f32))[:HD].astype(bf16)
        grad_t = jnp.transpose(grad_wide)[:HD].astype(bf16)
        key_part = mm(query_t, score_grad)
        value_part = mm(grad_t, probs.astype(bf16))
        if j == 0:
            sums[:HD] = key_part
            sums[HD:] = value_part
        else:
            sums[:HD] = sums[:HD] + key_part
            sums[HD:] = sums[HD:] + value_part
    query_sum, value_sum = None, None
    for j in range(blocks):
        lines = slice(j * rows, (j + 1) * rows)
        both = jnp.transpose(sums[:, lines])
        query_grad = query_grads[lines]
        outs[j][0, :rows] = jnp.where(low, query_grad, swap(both)).astype(bf16)
        outs[j][0, rows:] = jnp.where(low_half, swap(both[:half]), both[half:]).astype(bf16)
        term = column_sum(query_grad.astype(bf16).astype(f32))
        query_sum = term if query_sum is None else query_sum + term
        term = column_sum(swap(both).astype(bf16).astype(f32))
        value_sum = term if value_sum is None else value_sum + term
    turned[:HD] = jnp.transpose(query_grads[...])[:HD].astype(bf16)
    turned[HD:] = sums[...].astype(bf16)

    @pl.when(pl.program_id(0) == 0)
    def _():
        weight_ref[...] = jnp.zeros_like(weight_ref)
        bias_ref[...] = jnp.zeros_like(bias_ref)

    weight_ref[...] = weight_ref[...] + mm(turned[...], norm_ref[0])
    bias_ref[0:1, :] = bias_ref[0:1, :] + query_sum
    bias_ref[1:2, :] = bias_ref[1:2, :] + value_sum


def project_kernel(n_context, place_ref, *refs):
    blocks = len(refs) - 5
    folded, (own_ref, far_ref, mixed_ref, part_ref, scratch) = refs[:blocks], refs[blocks:]
    y = place_ref[2]
    images, half, _ = folded[0].shape
    rows = 2 * half
    for slot in range(blocks):
        scratch[owner_of(place_ref, slot, n_context)] = folded[slot][...]
    low = low_lanes((half, LANES))
    for pair in range(blocks // 2):
        columns = slice(pair * LANES, (pair + 1) * LANES)
        for image in range(images):
            first = scratch[2 * pair, image].astype(f32)
            second = scratch[2 * pair + 1, image].astype(f32)
            start = image * rows
            mixed_ref[start : start + half, columns] = jnp.where(
                low, first, swap(second)
            ).astype(bf16)
            mixed_ref[start + half : start + rows, columns] = jnp.where(
                low, swap(first), second
            ).astype(bf16)
    size = mixed_ref.shape[1] // 2
    total = None
    for group, ref in ((y, own_ref), (1 - y, far_ref)):
        mixed = mixed_ref[:, pl.ds(pl.multiple_of(group * size, LANES), size)]
        term = mm(mixed, ref[...], NT)
        total = term if total is None else total + term
    part_ref[...] = total.astype(bf16)


def norm_kernel(place_ref, x_ref, part_ref, other_ref, vec_ref, norm_ref, half_ref):
    vec = vec_ref[...]
    branch = part_ref[...].astype(f32) + other_ref[...].astype(f32) + row(vec, B_OUT)
    middle = x_ref[...].astype(f32) + row(vec, SCALE1) * branch
    normed, _ = normalise(middle)
    norm_ref[...] = (normed * row(vec, GAIN2) + row(vec, SHIFT2)).astype(bf16)
    half = half_ref.shape[0]
    half_ref[...] = norm_ref[pl.ds(pl.multiple_of(place_ref[3] * half, 16), half), :]


def mlp_kernel(
    place_ref, own_ref, near_ref, far_ref, cot_ref, vec_ref, bup_ref, weight_ref,
    norm_ref, grad_ref, act_ref, pre_ref, gup_ref, *refs
):
    outs, sums = refs[:4], refs[4]
    y, core = place_ref[2], place_ref[3]
    tokens, half = own_ref.shape[0], near_ref.shape[0]
    images = cot_ref.shape[0]
    rows = tokens // images
    mine = pl.multiple_of(core * half, 16)
    other = pl.multiple_of((1 - core) * half, 16)
    norm_ref[:tokens] = own_ref[...]
    norm_ref[pl.ds(tokens + mine, half), :] = near_ref[...]
    norm_ref[pl.ds(tokens + other, half), :] = far_ref[...]
    scale = vec_ref[SCALE2 : SCALE2 + 1, :]
    for yr in range(2):
        first = pl.multiple_of((y if yr == 0 else 1 - y) * rows, 16)
        for image in range(images):
            start = yr * tokens + image * rows
            value = scale * cot_ref[image, pl.ds(first, rows), :].astype(f32)
            grad_ref[start : start + rows] = value.astype(bf16)
    norm_low, branch_grad = norm_ref[...], grad_ref[...]
    hidden = bup_ref.shape[1]
    first = weight_ref.shape[1] - 2 * hidden
    step = hidden // 4
    down, back = None, None
    for part in range(4):
        columns = slice(part * step, (part + 1) * step)
        up = weight_ref[:, first + part * step : first + (part + 1) * step]
        start = first + hidden + part * step
        turned = weight_ref[:, start : start + step]
        pre = mm(norm_low, up) + bup_ref[:, columns]
        erf_term = 0.5 * (1.0 + lax.erf(pre * root_half))
        act = (pre * erf_term).astype(bf16)
        act_ref[:, columns] = act
        term = mm(act, turned, NT)
        down = term if down is None else down + term
        slope = erf_term + pre * inv_root_two_pi * jnp.exp(-0.5 * pre * pre)
        pre_grad = (mm(branch_grad, turned) * slope).astype(bf16)
        pre_ref[:, columns] = pre_grad
        gup_ref[:, columns] = column_sum(pre_grad.astype(f32))
        term = mm(pre_grad, up, NT)
        back = term if back is None else back + term
    for kind, value in ((0, back), (1, down)):
        sums[...] = value.astype(bf16)
        for out, spot in ((outs[2 * kind], mine), (outs[2 * kind + 1], other)):
            out[:half] = sums[pl.ds(spot, half), :]
            out[half:] = sums[pl.ds(tokens + spot, half), :]


def mlp_weights_kernel(norm_ref, grad_ref, act_ref, pre_ref, out_ref, norm_t, grad_t):
    kind = pl.program_id(0)

    @pl.when((kind == 0) & (pl.program_id(1) == 0))
    def _():
        norm_t[...] = turn(norm_ref[...])
        grad_t[...] = turn(grad_ref[...])

    @pl.when(kind == 0)
    def _():
        out_ref[...] = mm(norm_t[...], pre_ref[...]).astype(bf16)

    @pl.when(kind == 1)
    def _():
        out_ref[...] = mm(grad_t[...], act_ref[...]).astype(bf16)


def by_core(core, near_ref, far_ref, whole):
    half = near_ref.shape[0]
    whole[pl.ds(pl.multiple_of(core * half, 16), half), :] = near_ref[...].astype(f32)
    whole[pl.ds(pl.multiple_of((1 - core) * half, 16), half), :] = far_ref[...].astype(f32)
    return whole[...]


def result_kernel(
    place_ref, x_ref, cot_ref, part_ref, other_ref, near_ref, far_ref, vec_ref,
    result_ref, sums_ref, whole,
):
    vec = vec_ref[...]
    branch = part_ref[...].astype(f32) + other_ref[...].astype(f32) + row(vec, B_OUT)
    middle = x_ref[...].astype(f32) + row(vec, SCALE1) * branch
    mlp = by_core(place_ref[3], near_ref, far_ref, whole) + row(vec, B_DOWN)
    result_ref[...] = (middle + row(vec, SCALE2) * mlp).astype(bf16)
    sums_ref[...] = jnp.zeros_like(sums_ref)
    sums_ref[0:1, :] = column_sum(cot_ref[...].astype(f32) * mlp)


def back_kernel(
    images, n_context, place_ref, x_ref, cot_ref, part_ref, other_ref, near_ref, far_ref,
    vec_ref, own_ref, distant_ref, *refs
):
    middle_grad_ref, proj_ref, sums_ref = refs[:3]
    outs, scratch, whole = refs[3:-2], refs[-2], refs[-1]
    y, core = place_ref[2], place_ref[3]
    tokens = x_ref.shape[0]
    vec = vec_ref[...]
    upstream = cot_ref[...].astype(f32)
    branch = part_ref[...].astype(f32) + other_ref[...].astype(f32) + row(vec, B_OUT)
    middle = x_ref[...].astype(f32) + row(vec, SCALE1) * branch
    normed, inv_std = normalise(middle)
    norm_grad = by_core(core, near_ref, far_ref, whole)
    middle_grad = upstream + norm_back(norm_grad * row(vec, GAIN2), normed, inv_std)
    middle_grad_ref[...] = middle_grad
    proj_wide = row(vec, SCALE1) * middle_grad
    proj = proj_wide.astype(bf16)
    proj_ref[...] = proj
    sums_ref[...] = jnp.zeros_like(sums_ref)
    for place, value in (
        (B_OUT, proj_wide),
        (B_DOWN, row(vec, SCALE2) * upstream),
        (GAIN2, norm_grad * normed),
        (SHIFT2, norm_grad),
        (SCALE1, middle_grad * branch),
    ):
        sums_ref[place : place + 1, :] = column_sum(value)
    rows = tokens // images
    half = rows // 2
    low = low_lanes((half, LANES))
    size = own_ref.shape[1]
    for group, ref in ((y, own_ref), (1 - y, distant_ref)):
        wide = mm(proj, ref[...])
        for pair in range(size // LANES):
            head = group * n_context + 2 * pair
            for image in range(images):
                block = wide[image * rows : (image + 1) * rows, pair * LANES : (pair + 1) * LANES]
                first, second = block[:half], block[half:]
                scratch[head, image] = jnp.where(low, first, swap(second)).astype(bf16)
                scratch[head + 1, image] = jnp.where(low, swap(first), second).astype(bf16)
    for slot in range(len(outs)):
        outs[slot][...] = scratch[owner_of(place_ref, slot, n_context)]


def out_weights_kernel(place_ref, proj_ref, mixed_ref, own_ref, far_ref):
    y = place_ref[2]
    columns = own_ref.shape[1]
    proj_t = turn(proj_ref[...])
    for group, ref in ((y, own_ref), (1 - y, far_ref)):
        mixed = mixed_ref[:, pl.ds(pl.multiple_of(group * columns, LANES), columns)]
        ref[...] = mm(proj_t, mixed).astype(bf16)


def qkv_back_kernel(n_context, place_ref, *refs):
    packs, (own_ref, far_ref, part_ref, scratch, grads) = refs[:-5], refs[-5:]
    y = place_ref[2]
    blocks = len(packs)
    images = packs[0].shape[0]
    rows = packs[0].shape[1] * 2 // 3
    half = rows // 2
    columns = grads.shape[3]
    for slot in range(blocks):
        scratch[owner_of(place_ref, slot, n_context)] = packs[slot][...]
    low = low_lanes((rows, LANES))
    low_half = low_lanes((half, LANES))
    total = None
    for group in range(2):
        for pair in range(columns // LANES):
            head = group * n_context + 2 * pair
            lanes = slice(pair * LANES, (pair + 1) * LANES)
            for image in range(images):
                first = scratch[head, image].astype(f32)
                second = scratch[head + 1, image].astype(f32)
                start = image * rows
                here = slice(start, start + rows)
                grads[group, 0, here, lanes] = jnp.where(
                    low, first[:rows], swap(second[:rows])
                ).astype(bf16)
                grads[group, 1, here, lanes] = jnp.where(
                    low, swap(first[:rows]), second[:rows]
                ).astype(bf16)
                grads[group, 2, start : start + half, lanes] = jnp.where(
                    low_half, first[rows:], swap(second[rows:])
                ).astype(bf16)
                grads[group, 2, start + half : start + rows, lanes] = jnp.where(
                    low_half, swap(first[rows:]), second[rows:]
                ).astype(bf16)
    for group, ref in ((y, own_ref), (1 - y, far_ref)):
        for part in range(3):
            term = mm(grads[group, part], ref[:, part * columns : (part + 1) * columns], NT)
            total = term if total is None else total + term
    part_ref[...] = total.astype(bf16)


def head_grads_kernel(place_ref, *refs):
    pieces, (out_ref, wout_ref, scratch) = refs[:-3], refs[-3:]
    z = place_ref[1]
    count = len(pieces)
    rows = out_ref.shape[0]
    for j in range(count):
        head = lax.rem(z + j, count)
        for part in range(3):
            start = pl.multiple_of(part * count * HD + head * HD, HD)
            scratch[pl.ds(start, HD), :] = pieces[j][part * HD : (part + 1) * HD].astype(f32)
    out_ref[...] = jnp.transpose(scratch[...])[:rows]
    for block in range(wout_ref.shape[0] // LANES):
        lines = slice(3 * HD + block * rows, 3 * HD + (block + 1) * rows)
        total = pieces[0][lines].astype(f32)
        for piece in pieces[1:]:
            total = total + piece[lines].astype(f32)
        wout_ref[block * LANES : (block + 1) * LANES, :] = jnp.transpose(total)


def finish_kernel(
    sizes, place_ref, x_ref, middle_grad_ref, part_ref, other_ref, vec_ref, sums_ref, extra_ref,
    gup_ref, gqv_ref, out_ref, own_ref, far_ref,
):
    n_shard, n_context, last = sizes
    x, z = place_ref[0], place_ref[1]
    width = x_ref.shape[1]
    piece_rows = width // (n_shard * n_context)
    norm_grad = part_ref[...].astype(f32) + other_ref[...].astype(f32)
    normed, inv_std = normalise(x_ref[...].astype(f32))
    gain = vec_ref[GAIN1 : GAIN1 + 1, :]
    out_ref[...] = (
        middle_grad_ref[...] + norm_back(norm_grad * gain, normed, inv_std)
    ).astype(bf16)
    line = lax.broadcasted_iota(jnp.int32, sums_ref.shape, 0)
    sums = jnp.where(line == GAIN1, column_sum(norm_grad * normed), sums_ref[...])
    sums = jnp.where(line == SHIFT1, column_sum(norm_grad), sums)
    sums = jnp.where(line == SCALE2, extra_ref[0:1, :], sums).astype(bf16)
    up = gup_ref[...]
    line = lax.broadcasted_iota(jnp.int32, (SMALL_ROWS, up.shape[1]), 0)
    column = lax.broadcasted_iota(jnp.int32, (SMALL_ROWS, up.shape[1]), 1) // HD
    up = jnp.where(column == line, up, 0.0).astype(bf16)
    line = lax.broadcasted_iota(jnp.int32, (SMALL_ROWS, LANES), 0)
    low = low_lanes((SMALL_ROWS, LANES))
    qv = jnp.where((line == z) & low, gqv_ref[0:1, :], 0.0)
    qv = (qv + jnp.where((line == n_context + z) & low, gqv_ref[1:2, :], 0.0)).astype(bf16)
    for xr in range(n_shard):
        for zr in range(n_context):
            sc = lax.rem(x - xr + n_shard, n_shard) * n_context
            sc = sc + lax.rem(z - zr + n_context, n_context)
            start = (xr * n_context + zr) * SMALL_ROWS
            lines = slice(start, start + SMALL_ROWS)
            entry = lax.broadcasted_iota(jnp.int32, (LANES, width), 0)
            column = lax.broadcasted_iota(jnp.int32, (LANES, width), 1)
            place = jnp.where(
                (entry < piece_rows) & (column == sc * piece_rows + entry), 1.0, 0.0
            ).astype(bf16)
            term = mm(sums, place, NT)
            own_ref[lines, :LANES] = term
            far_ref[lines, :] = term
            own_ref[lines, LANES : 2 * LANES] = mm(up, spread_mask(sc, last, up.shape[1]), NT)
            own_ref[lines, 2 * LANES :] = mm(qv, spread_mask(sc, last, LANES), NT)


def merge_kernel(place_ref, own_ref, near_ref, far_ref, out_ref):
    y, core, image = place_ref[2], place_ref[3], pl.program_id(0)
    half = near_ref.shape[0]
    rows = own_ref.shape[0]
    block = rows // 2
    out_ref[0, pl.ds(pl.multiple_of(y * rows, 16), rows), :] = own_ref[...].astype(f32)
    for part in range(2):
        first = image * rows + part * block
        source = first // half
        line = pl.multiple_of(first - source * half, 16)
        there = pl.multiple_of((1 - y) * rows + part * block, 16)

        @pl.when(source == core)
        def _():
            out_ref[0, pl.ds(there, block), :] = near_ref[pl.ds(line, block), :].astype(f32)

        @pl.when(source != core)
        def _():
            out_ref[0, pl.ds(there, block), :] = far_ref[pl.ds(line, block), :].astype(f32)


KERNEL_US = {
    "bundle": 3,
    "prepare": 2,
    "attend": 26,
    "project": 4,
    "norm": 4,
    "mlp": 19,
    "mlp_weights": 12,
    "back": 8,
    "out_weights": 3,
    "result": 6,
    "attend_back": 26,
    "qkv_back": 6,
    "finish": 6,
    "head_grads": 2,
    "merge": 4,
}


def cost_of(name):
    time = KERNEL_US[name]
    return pl.CostEstimate(
        flops=int(time * FLOPS), transcendentals=0, bytes_accessed=int(time * BYTES)
    )


def vmem():
    return pl.BlockSpec(memory_space=pltpu.VMEM)


def smem():
    return pl.BlockSpec(memory_space=pltpu.SMEM)


def shaped(shape, dtype):
    return jax.ShapeDtypeStruct(shape, dtype)


def call(kernel, name, out_shape, scratch, place, *operands):
    return pl.pallas_call(
        kernel,
        name=name,
        cost_estimate=cost_of(name),
        in_specs=[smem()] + [vmem()] * len(operands),
        out_specs=[vmem()] * len(out_shape),
        out_shape=out_shape,
        scratch_shapes=scratch,
    )(place, *operands)


def per_device(sizes, *args):
    (
        tokens_in,
        counts,
        w_qkv,
        b_qv,
        w_out,
        b_out,
        w_up,
        b_up,
        w_down,
        b_down,
        norm1_gain,
        norm1_bias,
        norm2_gain,
        norm2_bias,
        scale1,
        scale2,
        cotangent,
    ) = args
    n_shard, n_context, n_y = sizes
    images, row_count, width = tokens_in.shape
    piece_rows = w_qkv.shape[0]
    head_columns = w_qkv.shape[2]
    hidden = w_up.shape[1]
    last = b_up.shape[1]
    rows = row_count // n_y
    half = rows // 2
    tokens = images * rows
    x = lax.axis_index("shard")
    z = lax.axis_index("context")
    y = lax.axis_index("y")
    core = lax.axis_index("core")
    place = jnp.stack([x, z, y, core]).astype(jnp.int32)
    blocks = n_y * n_context
    everyone = ("shard", "context")

    def send(value, axis, step):
        size = {"shard": n_shard, "context": n_context}[axis]
        return lax.ppermute(value, axis, [(i, (i + step) % size) for i in range(size)])

    def across(value):
        return lax.ppermute(value, "y", [(0, 1), (1, 0)])

    def partner(value):
        return lax.ppermute(value, "core", [(0, 1), (1, 0)])

    def hand_over(values, back):
        out = [values[0]]
        for slot in range(1, blocks):
            jy, jz = slot // n_context, slot % n_context
            step = -jz if back else jz
            pairs = [
                (i * n_y + t, (i + step) % n_context * n_y + (t ^ jy))
                for i in range(n_context)
                for t in range(n_y)
            ]
            out.append(lax.ppermute(values[slot], ("context", "y"), pairs))
        return out

    flat_qkv = w_qkv.reshape(piece_rows, -1)
    attention = lax.all_gather(
        jnp.concatenate([flat_qkv, w_out.T], axis=1), everyone, axis=0, tiled=True
    )
    feed = lax.all_gather(
        jnp.concatenate([w_up, w_down.T], axis=1), everyone, axis=0, tiled=True
    )

    vectors = [b_out, b_down, norm1_gain, norm1_bias, norm2_gain, norm2_bias, scale1, scale2]

    def block_of(value):
        return jnp.pad(value, ((0, SMALL_ROWS - value.shape[0]), (0, LANES - value.shape[1])))

    small = jnp.concatenate(
        [block_of(jnp.stack(vectors)), block_of(b_up), block_of(b_qv.reshape(-1, last))], axis=0
    )
    step_rows = piece_rows + 3 * SMALL_ROWS
    quarter_rows = half
    quarter = images * quarter_rows
    block = block_rows(step_rows)
    bundles = call(
        bundle_kernel,
        "bundle",
        [shaped((block, width), bf16)]
        + [shaped((quarter + block, width), bf16)] * (n_context - 1),
        [pltpu.VMEM((n_context, block, width), bf16)],
        place,
        flat_qkv,
        small,
        tokens_in,
    )
    near = [send(bundles[j], "context", j) for j in range(1, n_context)]
    head_stack = jnp.concatenate([bundles[0]] + [value[quarter:] for value in near], axis=0)
    head_stacks = [head_stack] + [send(head_stack, "shard", j) for j in range(1, n_shard)]
    def after(value, *others):
        return lax.optimization_barrier((value, *others))[0]

    weight_head, vec, bias_head, bup = call(
        functools.partial(prepare_kernel, (n_shard, n_context, last, b_qv.shape[1])),
        "prepare",
        [
            shaped((width, 2 * LANES), bf16),
            shaped((SMALL_ROWS, width), f32),
            shaped((8, 2 * LANES), f32),
            shaped((1, hidden), f32),
        ],
        [],
        place,
        *head_stacks,
    )

    quarters = []
    for j, value in enumerate(near):
        value = value[:quarter]
        far = across(value)
        crossed = after(far, weight_head) if j + 1 == n_context // 2 else far
        quarters += [value, far, partner(value), partner(crossed)]
    wout = attention[:, 3 * head_columns :]
    wout_far = across(after(wout, *quarters))
    def own_rows(array):
        return lax.dynamic_slice_in_dim(array, y * rows, rows, 1).reshape(tokens, width)

    residual = own_rows(tokens_in)
    upstream = own_rows(cotangent)

    pack_rows = rows + half
    slot = jnp.arange(blocks)
    source = (z - slot % n_context) % n_context * row_count + (y ^ (slot // n_context)) * rows
    key_place = (source[:, None] + jnp.arange(rows)[None, :]).reshape(1, -1).astype(jnp.int32)
    length = blocks * rows
    pack_spec = pl.BlockSpec((1, pack_rows, LANES), lambda i: (i, 0, 0))
    fold_spec = pl.BlockSpec((1, half, LANES), lambda i: (i, 0, 0))
    pos_spec = pl.BlockSpec((1, length), lambda i: (0, 0))
    log_spec = pl.BlockSpec((1, length, 1), lambda i: (i, 0, 0))
    head_spec = pl.BlockSpec((1, length, LANES), lambda i: (i, 0, 0))
    norm_spec = pl.BlockSpec((1, length, width), lambda i: (i, 0, 0))

    def fixed(shape):
        return pl.BlockSpec(shape, lambda i: (0,) * len(shape))

    attended = pl.pallas_call(
        functools.partial(attend_kernel, n_context),
        name="attend",
        cost_estimate=cost_of("attend"),
        grid=(images,),
        in_specs=[smem(), smem(), pos_spec]
        + [fixed((width, 2 * LANES)), fixed((SMALL_ROWS, width)), fixed((8, 2 * LANES))]
        + [pl.BlockSpec((1, row_count, width), lambda i: (i, 0, 0))]
        + [pl.BlockSpec((quarter_rows, width), lambda i: (i, 0))] * len(quarters),
        out_specs=[fold_spec] * blocks + [log_spec, norm_spec, head_spec, head_spec],
        out_shape=[shaped((images, half, LANES), bf16)] * blocks
        + [
            shaped((images, length, 1), f32),
            shaped((images, length, width), bf16),
            shaped((images, length, LANES), bf16),
            shaped((images, length, LANES), bf16),
        ],
        scratch_shapes=[pltpu.VMEM((length, LANES), bf16), pltpu.VMEM((rows, width), bf16)],
    )(counts, place, key_place, weight_head, vec, bias_head, tokens_in, *quarters)
    mixes, (log_total, norm_all, head_qk, head_v) = attended[:blocks], attended[blocks:]
    folded = hand_over(mixes, True)

    fold_scratch = pltpu.VMEM((blocks, images, half, LANES), bf16)
    mixture, proj_part = call(
        functools.partial(project_kernel, n_context),
        "project",
        [shaped((tokens, blocks * HD), bf16), shaped((tokens, width), bf16)],
        [fold_scratch],
        place,
        *folded,
        wout,
        wout_far,
    )
    proj_other = partner(proj_part)

    core_rows = tokens // CORES
    norm_own, norm_half = call(
        norm_kernel,
        "norm",
        [shaped((tokens, width), bf16), shaped((core_rows, width), bf16)],
        [],
        place,
        residual,
        proj_part,
        proj_other,
        vec,
    )
    norm_near = across(norm_half)
    norm_far = partner(norm_near)
    wqkv = after(attention[:, : 3 * head_columns], norm_near)
    wqkv_far = across(wqkv)
    mlp_rows = n_y * tokens
    (norm_low2, branch_grad, hidden_act, pre_grad, grad_bup, *halves) = call(
        mlp_kernel,
        "mlp",
        [
            shaped((mlp_rows, width), bf16),
            shaped((mlp_rows, width), bf16),
            shaped((mlp_rows, hidden), bf16),
            shaped((mlp_rows, hidden), bf16),
            shaped((1, hidden), f32),
        ]
        + [shaped((tokens, width), bf16)] * 4,
        [pltpu.VMEM((mlp_rows, width), bf16)],
        place,
        norm_own,
        norm_near,
        norm_far,
        cotangent,
        vec,
        bup,
        feed,
    )

    def sum_cores(mine, given):
        return (mine.astype(f32) + partner(given).astype(f32)).astype(bf16)

    def sum_y(both):
        part = both[:core_rows].astype(f32) + across(both[core_rows:]).astype(f32)
        return part.astype(bf16)

    back_both = sum_cores(halves[0], halves[1])
    back_half = sum_y(back_both)
    hidden_act = after(hidden_act, back_both)
    steps = 2
    columns = hidden // steps
    whole_spec = pl.BlockSpec((mlp_rows, width), lambda i, k: (0, 0))
    feed_grad = pl.pallas_call(
        mlp_weights_kernel,
        name="mlp_weights",
        cost_estimate=cost_of("mlp_weights"),
        grid=(2, steps),
        in_specs=[
            whole_spec,
            whole_spec,
            pl.BlockSpec((mlp_rows, columns), lambda i, k: (0, i * k)),
            pl.BlockSpec((mlp_rows, columns), lambda i, k: (0, (1 - i) * k + i * (steps - 1))),
        ],
        out_specs=pl.BlockSpec((width, columns), lambda i, k: (0, i * steps + k)),
        out_shape=shaped((width, 2 * hidden), bf16),
        scratch_shapes=[pltpu.VMEM((width, mlp_rows), bf16)] * 2,
    )(norm_low2, branch_grad, hidden_act, pre_grad)
    back_half, feed_grad = lax.optimization_barrier((back_half, feed_grad))
    back_far = partner(back_half)
    feed_grad = lax.psum_scatter(feed_grad, everyone, scatter_dimension=0, tiled=True)

    back = call(
        functools.partial(back_kernel, images, n_context),
        "back",
        [
            shaped((tokens, width), f32),
            shaped((tokens, width), bf16),
            shaped((SMALL_ROWS, width), f32),
        ]
        + [shaped((images, half, LANES), bf16)] * blocks,
        [fold_scratch, pltpu.VMEM((tokens, width), f32)],
        place,
        residual,
        upstream,
        proj_part,
        proj_other,
        back_half,
        back_far,
        vec,
        wout,
        wout_far,
    )
    middle_grad, proj_grad, sums = back[:3]
    mix_grads = hand_over(back[3:], False)
    out_own, out_far = call(
        out_weights_kernel,
        "out_weights",
        [shaped((width, head_columns), bf16)] * 2,
        [],
        place,
        proj_grad,
        mixture,
    )

    down_half = sum_y(sum_cores(after(halves[2], back_half), halves[3]))
    down_half = after(down_half, proj_grad)
    result, extra = call(
        result_kernel,
        "result",
        [shaped((tokens, width), bf16), shaped((8, width), f32)],
        [pltpu.VMEM((tokens, width), f32)],
        place,
        residual,
        upstream,
        proj_part,
        proj_other,
        down_half,
        partner(down_half),
        vec,
    )

    mix_grads = lax.optimization_barrier((out_own, out_far, result, extra, *mix_grads))
    out_own, out_far, result, extra = mix_grads[:4]
    mix_grads = mix_grads[4:]
    attended_back = pl.pallas_call(
        attend_back_kernel,
        name="attend_back",
        cost_estimate=cost_of("attend_back"),
        grid=(images,),
        in_specs=[smem(), pos_spec, log_spec, norm_spec, head_spec, head_spec]
        + [fold_spec] * (2 * blocks),
        out_specs=[pack_spec] * blocks + [fixed((3 * HD, width)), fixed((8, LANES))],
        out_shape=[shaped((images, pack_rows, LANES), bf16)] * blocks
        + [shaped((3 * HD, width), f32), shaped((8, LANES), f32)],
        scratch_shapes=[
            pltpu.VMEM((length, LANES), bf16),
            pltpu.VMEM((2 * HD, length), f32),
            pltpu.VMEM((length, LANES), f32),
            pltpu.VMEM((3 * HD, length), bf16),
        ],
    )(counts, key_place, log_total, norm_all, head_qk, head_v, *mixes, *mix_grads)
    grad_head, grad_qv = attended_back[blocks:]
    pack_grads = hand_over(attended_back[:blocks], True)

    part_rows = n_context * piece_rows
    def whole_rows(value):
        mine = lax.dynamic_slice_in_dim(value, core * (tokens // 2), tokens // 2, 0)
        near = across(mine)
        far = partner(near)
        half_spec = pl.BlockSpec((tokens // 2, width), lambda i: (0, 0))
        return pl.pallas_call(
            merge_kernel,
            name="merge",
        cost_estimate=cost_of("merge"),
            grid=(images,),
            in_specs=[smem(), pl.BlockSpec((rows, width), lambda i: (i, 0)), half_spec, half_spec],
            out_specs=pl.BlockSpec((1, row_count, width), lambda i: (i, 0, 0)),
            out_shape=shaped((images, row_count, width), f32),
        )(place, value, near, far)

    pack_grads = lax.optimization_barrier(
        (
            feed_grad[:, :hidden].astype(f32),
            feed_grad[:, hidden:].astype(f32).T,
            *pack_grads,
        )
    )
    grad_wup, grad_wdown = pack_grads[:2]
    pack_grads = pack_grads[2:]
    (norm1_part,) = call(
        functools.partial(qkv_back_kernel, n_context),
        "qkv_back",
        [shaped((tokens, width), bf16)],
        [
            pltpu.VMEM((blocks, images, pack_rows, LANES), bf16),
            pltpu.VMEM((n_y, 3, tokens, head_columns), bf16),
        ],
        place,
        *pack_grads,
        wqkv,
        wqkv_far,
    )
    norm1_other = partner(norm1_part)

    input_grad, own, far = call(
        functools.partial(finish_kernel, (n_shard, n_context, last)),
        "finish",
        [shaped((tokens, width), bf16)]
        + [
            shaped((n_shard * n_context * SMALL_ROWS, SMALL_LANES), f32),
            shaped((n_shard * n_context * SMALL_ROWS, LANES), f32),
        ],
        [],
        place,
        residual,
        middle_grad,
        norm1_part,
        norm1_other,
        vec,
        sums,
        extra,
        grad_bup,
        grad_qv,
    )
    far = jnp.pad(across(far), ((0, 0), (0, SMALL_LANES - LANES)))
    total = (own + far).reshape(n_shard, -1, SMALL_LANES)
    over_shard = total[0]
    for j in range(1, n_shard):
        over_shard = over_shard + send(total[j], "shard", -j)
    over_shard = over_shard.reshape(n_context, SMALL_ROWS, SMALL_LANES)
    small_grad = over_shard[0]
    for j in range(1, n_context):
        small_grad = small_grad + send(over_shard[j], "context", -j)

    out_sum = (out_own.astype(f32) + across(out_far).astype(f32)).astype(bf16)
    grad_head, out_sum = lax.optimization_barrier(
        (grad_head, out_sum, norm1_part)
    )[:2]

    def shard_part(j):
        start = lax.rem(x - j + n_shard, n_shard) * part_rows
        head = lax.dynamic_slice_in_dim(grad_head, start, part_rows, 1).astype(bf16)
        rest = lax.dynamic_slice_in_dim(out_sum, start, part_rows, 0)
        wide = part_rows // head_columns
        if wide > 1:
            rest = jnp.concatenate(jnp.split(rest, wide, axis=0), axis=1)
        else:
            rest = jnp.concatenate(jnp.split(rest, head_columns // part_rows, axis=1), axis=0)
        return jnp.concatenate([head, rest], axis=0)

    both = shard_part(0).astype(f32)
    for j in range(1, n_shard):
        both = both + send(shard_part(j), "shard", -j).astype(f32)
    both = after(both.astype(bf16), input_grad)
    head_sum, out_sum = both[: 3 * HD], both[3 * HD :]
    if part_rows > head_columns:
        out_sum = jnp.concatenate(jnp.split(out_sum, part_rows // head_columns, axis=1), axis=0)
    else:
        out_sum = jnp.concatenate(jnp.split(out_sum, head_columns // part_rows, axis=0), axis=1)
    lane_pad = -piece_rows % LANES

    def context_part(j):
        start = lax.rem(z - j + n_context, n_context) * piece_rows
        head = lax.dynamic_slice_in_dim(head_sum, start, piece_rows, 1)
        rest = lax.dynamic_slice_in_dim(out_sum, start, piece_rows, 0)
        rest = jnp.concatenate(jnp.split(rest, head_columns // LANES, axis=1), axis=0)
        return jnp.concatenate([jnp.pad(head, ((0, 0), (0, lane_pad))), rest], axis=0)

    parts = [context_part(0)]
    for j in range(1, n_context):
        parts.append(send(context_part(j), "context", -j))
    grad_wqkv, grad_wout = call(
        head_grads_kernel,
        "head_grads",
        [shaped((piece_rows, 3 * head_columns), f32), shaped((head_columns, piece_rows), f32)],
        [pltpu.VMEM((3 * head_columns, piece_rows + lane_pad), f32)],
        place,
        *parts,
    )
    vec_grad = small_grad[: len(vectors), :piece_rows]
    return (
        whole_rows(result),
        whole_rows(input_grad),
        grad_wqkv.reshape(piece_rows, 3, head_columns),
        small_grad[: b_qv.shape[0] * b_qv.shape[1], 2 * LANES : 2 * LANES + last].reshape(
            b_qv.shape
        ),
        grad_wout,
        vec_grad[B_OUT],
        grad_wup,
        small_grad[: b_up.shape[0], LANES : LANES + last],
        grad_wdown,
        vec_grad[B_DOWN],
        vec_grad[GAIN1],
        vec_grad[SHIFT1],
        vec_grad[GAIN2],
        vec_grad[SHIFT2],
        vec_grad[SCALE1],
        vec_grad[SCALE2],
    )


def solution(mesh):
    pair = ("y", "core")
    both = ("shard", "context")
    tokens = P("shard", "context", None)
    vector = P(both)
    in_specs = (
        tokens,
        P("shard"),
        P(both, None, pair),
        P(None, pair, both),
        P(pair, both),
        vector,
        P(both, pair),
        P(pair, both),
        P(pair, both),
    ) + (vector,) * 7
    in_specs = in_specs + (tokens,)
    out_specs = (
        tokens,
        tokens,
        P(both, None, pair),
        P(None, pair, both),
        P(pair, both),
        vector,
        P(both, pair),
        P(pair, both),
        P(pair, both),
    ) + (vector,) * 7
    sizes = tuple(mesh.shape[name] for name in ("shard", "context", "tensor"))
    split = Mesh(
        mesh.devices.reshape(sizes[0], sizes[1], sizes[2] // CORES, CORES),
        ("shard", "context", "y", "core"),
    )
    return jax.shard_map(
        functools.partial(per_device, split.devices.shape[:3]),
        mesh=split,
        in_specs=in_specs,
        out_specs=out_specs,
        check_vma=False,
    )
```

```python
import functools

import jax
import jax.numpy as jnp
from jax import lax
from jax.experimental import pallas as pl
from jax.experimental.pallas import tpu as pltpu
from jax.sharding import Mesh
from jax.sharding import PartitionSpec as P

HD = 64
LANES = 128
CORES = 2
SMALL_ROWS = 16
SMALL_LANES = 3 * LANES
FLOPS, BYTES = 1e+09, 3e+06

eps_norm = 1e-06
masked_score = -1e30
root_half = 0.7071067811865476
inv_root_two_pi = 0.3989422804014327
score_scale = HD ** (-0.5)

bf16 = jnp.bfloat16
f32 = jnp.float32
NN = (((1,), (0,)), ((), ()))
NT = (((1,), (1,)), ((), ()))

B_OUT, B_DOWN, GAIN1, SHIFT1, GAIN2, SHIFT2, SCALE1, SCALE2 = range(8)


def mm(left, right, dims=NN):
    return lax.dot_general(left, right, dims, preferred_element_type=f32)


def turn(values):
    return jnp.transpose(values.astype(f32)).astype(bf16)


def normalise(values):
    average = jnp.mean(values, axis=-1, keepdims=True)
    centred = values - average
    variance = jnp.mean(centred * centred, axis=-1, keepdims=True)
    inv_std = lax.rsqrt(variance + eps_norm)
    return centred * inv_std, inv_std


def norm_back(grad_in, normed, inv_std):
    first_mean = jnp.mean(grad_in, axis=-1, keepdims=True)
    second_mean = jnp.mean(grad_in * normed, axis=-1, keepdims=True)
    return inv_std * (grad_in - first_mean - normed * second_mean)


def row(table, index):
    return table[index : index + 1, :]


def column_sum(values):
    return jnp.sum(values, axis=0, keepdims=True)


def low_lanes(shape):
    return lax.broadcasted_iota(jnp.int32, shape, 1) < HD


def swap(values):
    return pltpu.roll(values, HD, 1)


def fold(wide):
    half = wide.shape[0] // 2
    return wide[:half] + swap(wide[half:])


def unfold(folded):
    low = low_lanes(folded.shape)
    return jnp.concatenate(
        [jnp.where(low, folded, 0.0), jnp.where(low, swap(folded), 0.0)], axis=0
    )


def owner_of(place_ref, slot, context):
    z, y = place_ref[1], place_ref[2]
    group = y if slot < context else 1 - y
    return group * context + lax.rem(z + slot % context, context)


def spread_mask(sc, last, columns):
    entry = lax.broadcasted_iota(jnp.int32, (LANES, columns), 0)
    column = lax.broadcasted_iota(jnp.int32, (LANES, columns), 1)
    return jnp.where(
        (entry < last) & (lax.rem(column, HD) == sc * last + entry), 1.0, 0.0
    ).astype(bf16)


def block_rows(step_rows):
    return -(-step_rows // (4 * SMALL_ROWS)) * SMALL_ROWS


def chunks_of(first, size, block):
    while size:
        count = min(size, block - first % block)
        yield first, count, first // block * 2 * LANES, first % block
        first, size = first + count, size - count


def bundle_kernel(place_ref, w_ref, small_ref, tokens_ref, own_ref, *refs):
    outs, scratch = refs[:-1], refs[-1]
    z, spot = place_ref[1], 2 * place_ref[2] + place_ref[3]
    rows = w_ref.shape[0]
    step_rows = rows + small_ref.shape[0]
    block = own_ref.shape[0]
    count = len(outs) + 1
    columns = w_ref.shape[1] // 3
    images, row_count, _ = tokens_ref.shape
    quarter = row_count // 4
    low = low_lanes((rows, LANES))
    scratch[...] = jnp.zeros_like(scratch)
    for head in range(count):
        first = head // 2 * LANES
        query, key, value = (
            w_ref[:, part * columns + first : part * columns + first + LANES].astype(f32)
            for part in range(3)
        )
        if head % 2:
            query, value = swap(query), swap(value)
        else:
            key = swap(key)
        both = jnp.where(low, query, key).astype(bf16)
        value = jnp.where(low, value, 0.0).astype(bf16)
        for start, size, lane, line in chunks_of(0, rows, block):
            here = slice(line, line + size)
            scratch[head, here, lane : lane + LANES] = both[start : start + size]
            scratch[head, here, lane + LANES : lane + 2 * LANES] = value[start : start + size]
        for start, size, lane, line in chunks_of(rows, step_rows - rows, block):
            here = slice(line, line + size)
            scratch[head, here, lane : lane + LANES] = small_ref[start - rows : start - rows + size]
    own_ref[...] = scratch[z]
    for j, out in enumerate(outs):
        for image in range(images):
            there = pl.ds(pl.multiple_of(spot * quarter, 16), quarter)
            out[image * quarter : (image + 1) * quarter, :] = tokens_ref[image, there, :]
        out[images * quarter :, :] = scratch[lax.rem(z + j + 1, count)]


def prepare_kernel(sizes, place_ref, *refs):
    n_shard, n_context, last, heads = sizes
    stacks = refs[:n_shard]
    weight_ref, vec_ref, bias_ref, bup_ref = refs[n_shard:]
    x, z = place_ref[0], place_ref[1]
    width = weight_ref.shape[0]
    piece_rows = width // (n_shard * n_context)
    block = stacks[0].shape[0] // n_context
    vec, qv, up = None, None, None
    for xr in range(n_shard):
        for zr in range(n_context):
            sc = lax.rem(x - xr + n_shard, n_shard) * n_context
            sc = sc + lax.rem(z - zr + n_context, n_context)
            stack = stacks[xr]
            base = pl.multiple_of(sc * piece_rows, 16)
            for start, size, lane, line in chunks_of(0, piece_rows, block):
                line = zr * block + line
                weight_ref[pl.ds(base + start, size), :] = stack[
                    line : line + size, lane : lane + 2 * LANES
                ]

            def small(index):
                start = piece_rows + index * SMALL_ROWS
                lane, line = start // block * 2 * LANES, zr * block + start % block
                return stack[line : line + SMALL_ROWS, lane : lane + LANES]

            entry = lax.broadcasted_iota(jnp.int32, (LANES, width), 0)
            column = lax.broadcasted_iota(jnp.int32, (LANES, width), 1)
            place = jnp.where(
                (entry < piece_rows) & (column == sc * piece_rows + entry), 1.0, 0.0
            ).astype(bf16)
            term = mm(small(0), place)
            vec = term if vec is None else vec + term
            term = mm(small(1), spread_mask(sc, last, bup_ref.shape[1]))
            up = term if up is None else up + term
            term = mm(small(2), spread_mask(sc, last, 2 * LANES))
            qv = term if qv is None else qv + term
    vec_ref[...] = vec
    line = lax.broadcasted_iota(jnp.int32, up.shape, 0)
    column = lax.broadcasted_iota(jnp.int32, up.shape, 1)
    bup_ref[...] = column_sum(jnp.where(column // HD == line, up, 0.0))
    line = lax.broadcasted_iota(jnp.int32, qv.shape, 0)
    column = lax.broadcasted_iota(jnp.int32, qv.shape, 1) // HD
    chosen = ((line == z) & (column == 0)) | ((line == heads + z) & (column == 2))
    bias_ref[...] = jnp.zeros_like(bias_ref)
    bias_ref[0:1, :] = column_sum(jnp.where(chosen, qv, 0.0))


def attend_kernel(
    n_context, count_ref, place_ref, pos_ref, weight_ref, vec_ref, bias_ref, own_ref, *refs
):
    blocks = 2 * n_context
    n_quarter = 4 * (n_context - 1)
    quarters = refs[:n_quarter]
    outs = refs[n_quarter : n_quarter + blocks]
    log_ref, norm_ref, qk_ref, v_ref, keys, tokens = refs[n_quarter + blocks :]
    y, core = place_ref[2], place_ref[3]
    rows = own_ref.shape[1] // 2
    half = rows // 2
    gain, shift = vec_ref[GAIN1 : GAIN1 + 1, :], vec_ref[SHIFT1 : SHIFT1 + 1, :]
    low = low_lanes((rows, LANES))
    for jz in range(n_context):
        for jy in range(2):
            slot = jy * n_context + jz
            lines = slice(slot * rows, (slot + 1) * rows)
            if jz == 0:
                first = pl.multiple_of((y if jy == 0 else 1 - y) * rows, 16)
                block = own_ref[0, pl.ds(first, rows), :]
            else:
                for other in range(2):
                    spot = core if other == 0 else 1 - core
                    first = pl.multiple_of(spot * half, 16)
                    quarter = quarters[4 * (jz - 1) + 2 * other + jy]
                    tokens[pl.ds(first, half), :] = quarter[...]
                block = tokens[...]
            normed, _ = normalise(block.astype(f32))
            norm_low = (normed * gain + shift).astype(bf16)
            norm_ref[0, lines, :] = norm_low
            qkv = mm(norm_low, weight_ref[...]) + bias_ref[0:1, :]
            qk_ref[0, lines, :] = qkv[:, :LANES].astype(bf16)
            v_ref[0, lines, :] = qkv[:, LANES:].astype(bf16)
            keys[lines, :] = jnp.where(low, swap(qkv[:, :LANES]), 0.0).astype(bf16)
    valid = pos_ref[...] < count_ref[pl.program_id(0)]
    for j in range(blocks):
        query = qk_ref[0, j * rows : (j + 1) * rows] * bf16(score_scale)
        scores = jnp.where(valid, mm(query, keys[...], NT), masked_score)
        highest = jnp.max(scores, axis=1, keepdims=True)
        exponent = jnp.exp(scores - highest)
        total = jnp.sum(exponent, axis=1, keepdims=True)
        mixed = mm(exponent.astype(bf16), v_ref[0]) / total
        outs[j][0] = fold(mixed).astype(bf16)
        log_ref[0, j * rows : (j + 1) * rows] = highest + jnp.log(total)


def attend_back_kernel(count_ref, pos_ref, log_ref, norm_ref, qk_ref, v_ref, *refs):
    blocks = (len(refs) - 6) // 3
    mixes, grads, outs = (refs[i * blocks : (i + 1) * blocks] for i in range(3))
    weight_ref, bias_ref, keys, sums, query_grads, turned = refs[3 * blocks :]
    rows = qk_ref.shape[1] // blocks
    half = rows // 2
    low = low_lanes((rows, LANES))
    low_half = low_lanes((half, LANES))
    for j in range(blocks):
        pack = qk_ref[0, j * rows : (j + 1) * rows].astype(f32)
        keys[j * rows : (j + 1) * rows] = jnp.where(low, swap(pack), 0.0).astype(bf16)
    valid = pos_ref[...] < count_ref[pl.program_id(0)]
    for j in range(blocks):
        lines = slice(j * rows, (j + 1) * rows)
        query = qk_ref[0, lines] * bf16(score_scale)
        grad_wide = unfold(grads[j][0].astype(f32))
        mix_wide = unfold(mixes[j][0].astype(f32))
        delta = jnp.sum(grad_wide * mix_wide, axis=1, keepdims=True)
        grad = grad_wide.astype(bf16)
        scores = jnp.where(valid, mm(query, keys[...], NT), masked_score)
        probs = jnp.exp(scores - log_ref[0, lines])
        weight_grad = mm(grad, v_ref[0], NT)
        score_grad = (probs * (weight_grad - delta)).astype(bf16)
        query_grads[lines] = mm(score_grad, keys[...]) * score_scale
        query_t = jnp.transpose(query.astype(f32))[:HD].astype(bf16)
        grad_t = jnp.transpose(grad_wide)[:HD].astype(bf16)
        key_part = mm(query_t, score_grad)
        value_part = mm(grad_t, probs.astype(bf16))
        if j == 0:
            sums[:HD] = key_part
            sums[HD:] = value_part
        else:
            sums[:HD] = sums[:HD] + key_part
            sums[HD:] = sums[HD:] + value_part
    query_sum, value_sum = None, None
    for j in range(blocks):
        lines = slice(j * rows, (j + 1) * rows)
        both = jnp.transpose(sums[:, lines])
        query_grad = query_grads[lines]
        outs[j][0, :rows] = jnp.where(low, query_grad, swap(both)).astype(bf16)
        outs[j][0, rows:] = jnp.where(low_half, swap(both[:half]), both[half:]).astype(bf16)
        term = column_sum(query_grad.astype(bf16).astype(f32))
        query_sum = term if query_sum is None else query_sum + term
        term = column_sum(swap(both).astype(bf16).astype(f32))
        value_sum = term if value_sum is None else value_sum + term
    turned[:HD] = jnp.transpose(query_grads[...])[:HD].astype(bf16)
    turned[HD:] = sums[...].astype(bf16)

    @pl.when(pl.program_id(0) == 0)
    def _():
        weight_ref[...] = jnp.zeros_like(weight_ref)
        bias_ref[...] = jnp.zeros_like(bias_ref)

    weight_ref[...] = weight_ref[...] + mm(turned[...], norm_ref[0])
    bias_ref[0:1, :] = bias_ref[0:1, :] + query_sum
    bias_ref[1:2, :] = bias_ref[1:2, :] + value_sum


def project_kernel(n_context, place_ref, *refs):
    blocks = len(refs) - 5
    folded, (own_ref, far_ref, mixed_ref, part_ref, scratch) = refs[:blocks], refs[blocks:]
    y = place_ref[2]
    images, half, _ = folded[0].shape
    rows = 2 * half
    for slot in range(blocks):
        scratch[owner_of(place_ref, slot, n_context)] = folded[slot][...]
    low = low_lanes((half, LANES))
    for pair in range(blocks // 2):
        columns = slice(pair * LANES, (pair + 1) * LANES)
        for image in range(images):
            first = scratch[2 * pair, image].astype(f32)
            second = scratch[2 * pair + 1, image].astype(f32)
            start = image * rows
            mixed_ref[start : start + half, columns] = jnp.where(
                low, first, swap(second)
            ).astype(bf16)
            mixed_ref[start + half : start + rows, columns] = jnp.where(
                low, swap(first), second
            ).astype(bf16)
    size = mixed_ref.shape[1] // 2
    total = None
    for group, ref in ((y, own_ref), (1 - y, far_ref)):
        mixed = mixed_ref[:, pl.ds(pl.multiple_of(group * size, LANES), size)]
        term = mm(mixed, ref[...], NT)
        total = term if total is None else total + term
    part_ref[...] = total.astype(bf16)


def norm_kernel(place_ref, x_ref, part_ref, other_ref, vec_ref, norm_ref, half_ref):
    vec = vec_ref[...]
    branch = part_ref[...].astype(f32) + other_ref[...].astype(f32) + row(vec, B_OUT)
    middle = x_ref[...].astype(f32) + row(vec, SCALE1) * branch
    normed, _ = normalise(middle)
    norm_ref[...] = (normed * row(vec, GAIN2) + row(vec, SHIFT2)).astype(bf16)
    half = half_ref.shape[0]
    half_ref[...] = norm_ref[pl.ds(pl.multiple_of(place_ref[3] * half, 16), half), :]


def mlp_kernel(
    place_ref, own_ref, near_ref, far_ref, cot_ref, vec_ref, bup_ref, weight_ref,
    norm_ref, grad_ref, act_ref, pre_ref, gup_ref, *refs
):
    outs, sums = refs[:4], refs[4]
    y, core = place_ref[2], place_ref[3]
    tokens, half = own_ref.shape[0], near_ref.shape[0]
    images = cot_ref.shape[0]
    rows = tokens // images
    mine = pl.multiple_of(core * half, 16)
    other = pl.multiple_of((1 - core) * half, 16)
    norm_ref[:tokens] = own_ref[...]
    norm_ref[pl.ds(tokens + mine, half), :] = near_ref[...]
    norm_ref[pl.ds(tokens + other, half), :] = far_ref[...]
    scale = vec_ref[SCALE2 : SCALE2 + 1, :]
    for yr in range(2):
        first = pl.multiple_of((y if yr == 0 else 1 - y) * rows, 16)
        for image in range(images):
            start = yr * tokens + image * rows
            value = scale * cot_ref[image, pl.ds(first, rows), :].astype(f32)
            grad_ref[start : start + rows] = value.astype(bf16)
    norm_low, branch_grad = norm_ref[...], grad_ref[...]
    hidden = bup_ref.shape[1]
    first = weight_ref.shape[1] - 2 * hidden
    step = hidden // 4
    down, back = None, None
    for part in range(4):
        columns = slice(part * step, (part + 1) * step)
        up = weight_ref[:, first + part * step : first + (part + 1) * step]
        start = first + hidden + part * step
        turned = weight_ref[:, start : start + step]
        pre = mm(norm_low, up) + bup_ref[:, columns]
        erf_term = 0.5 * (1.0 + lax.erf(pre * root_half))
        act = (pre * erf_term).astype(bf16)
        act_ref[:, columns] = act
        term = mm(act, turned, NT)
        down = term if down is None else down + term
        slope = erf_term + pre * inv_root_two_pi * jnp.exp(-0.5 * pre * pre)
        pre_grad = (mm(branch_grad, turned) * slope).astype(bf16)
        pre_ref[:, columns] = pre_grad
        gup_ref[:, columns] = column_sum(pre_grad.astype(f32))
        term = mm(pre_grad, up, NT)
        back = term if back is None else back + term
    for kind, value in ((0, back), (1, down)):
        sums[...] = value.astype(bf16)
        for out, spot in ((outs[2 * kind], mine), (outs[2 * kind + 1], other)):
            out[:half] = sums[pl.ds(spot, half), :]
            out[half:] = sums[pl.ds(tokens + spot, half), :]


def mlp_weights_kernel(norm_ref, grad_ref, act_ref, pre_ref, out_ref, norm_t, grad_t):
    kind = pl.program_id(0)

    @pl.when((kind == 0) & (pl.program_id(1) == 0))
    def _():
        norm_t[...] = turn(norm_ref[...])
        grad_t[...] = turn(grad_ref[...])

    @pl.when(kind == 0)
    def _():
        out_ref[...] = mm(norm_t[...], pre_ref[...]).astype(bf16)

    @pl.when(kind == 1)
    def _():
        out_ref[...] = mm(grad_t[...], act_ref[...]).astype(bf16)


def by_core(core, near_ref, far_ref, whole):
    half = near_ref.shape[0]
    whole[pl.ds(pl.multiple_of(core * half, 16), half), :] = near_ref[...].astype(f32)
    whole[pl.ds(pl.multiple_of((1 - core) * half, 16), half), :] = far_ref[...].astype(f32)
    return whole[...]


def result_kernel(
    place_ref, x_ref, cot_ref, part_ref, other_ref, near_ref, far_ref, vec_ref,
    result_ref, sums_ref, whole,
):
    vec = vec_ref[...]
    branch = part_ref[...].astype(f32) + other_ref[...].astype(f32) + row(vec, B_OUT)
    middle = x_ref[...].astype(f32) + row(vec, SCALE1) * branch
    mlp = by_core(place_ref[3], near_ref, far_ref, whole) + row(vec, B_DOWN)
    result_ref[...] = (middle + row(vec, SCALE2) * mlp).astype(bf16)
    sums_ref[...] = jnp.zeros_like(sums_ref)
    sums_ref[0:1, :] = column_sum(cot_ref[...].astype(f32) * mlp)


def back_kernel(
    images, n_context, place_ref, x_ref, cot_ref, part_ref, other_ref, near_ref, far_ref,
    vec_ref, own_ref, distant_ref, *refs
):
    middle_grad_ref, proj_ref, sums_ref = refs[:3]
    outs, scratch, whole = refs[3:-2], refs[-2], refs[-1]
    y, core = place_ref[2], place_ref[3]
    tokens = x_ref.shape[0]
    vec = vec_ref[...]
    upstream = cot_ref[...].astype(f32)
    branch = part_ref[...].astype(f32) + other_ref[...].astype(f32) + row(vec, B_OUT)
    middle = x_ref[...].astype(f32) + row(vec, SCALE1) * branch
    normed, inv_std = normalise(middle)
    norm_grad = by_core(core, near_ref, far_ref, whole)
    middle_grad = upstream + norm_back(norm_grad * row(vec, GAIN2), normed, inv_std)
    middle_grad_ref[...] = middle_grad
    proj_wide = row(vec, SCALE1) * middle_grad
    proj = proj_wide.astype(bf16)
    proj_ref[...] = proj
    sums_ref[...] = jnp.zeros_like(sums_ref)
    for place, value in (
        (B_OUT, proj_wide),
        (B_DOWN, row(vec, SCALE2) * upstream),
        (GAIN2, norm_grad * normed),
        (SHIFT2, norm_grad),
        (SCALE1, middle_grad * branch),
    ):
        sums_ref[place : place + 1, :] = column_sum(value)
    rows = tokens // images
    half = rows // 2
    low = low_lanes((half, LANES))
    size = own_ref.shape[1]
    for group, ref in ((y, own_ref), (1 - y, distant_ref)):
        wide = mm(proj, ref[...])
        for pair in range(size // LANES):
            head = group * n_context + 2 * pair
            for image in range(images):
                block = wide[image * rows : (image + 1) * rows, pair * LANES : (pair + 1) * LANES]
                first, second = block[:half], block[half:]
                scratch[head, image] = jnp.where(low, first, swap(second)).astype(bf16)
                scratch[head + 1, image] = jnp.where(low, swap(first), second).astype(bf16)
    for slot in range(len(outs)):
        outs[slot][...] = scratch[owner_of(place_ref, slot, n_context)]


def out_weights_kernel(place_ref, proj_ref, mixed_ref, own_ref, far_ref):
    y = place_ref[2]
    columns = own_ref.shape[1]
    proj_t = turn(proj_ref[...])
    for group, ref in ((y, own_ref), (1 - y, far_ref)):
        mixed = mixed_ref[:, pl.ds(pl.multiple_of(group * columns, LANES), columns)]
        ref[...] = mm(proj_t, mixed).astype(bf16)


def qkv_back_kernel(n_context, place_ref, *refs):
    packs, (own_ref, far_ref, part_ref, scratch, grads) = refs[:-5], refs[-5:]
    y = place_ref[2]
    blocks = len(packs)
    images = packs[0].shape[0]
    rows = packs[0].shape[1] * 2 // 3
    half = rows // 2
    columns = grads.shape[3]
    for slot in range(blocks):
        scratch[owner_of(place_ref, slot, n_context)] = packs[slot][...]
    low = low_lanes((rows, LANES))
    low_half = low_lanes((half, LANES))
    total = None
    for group in range(2):
        for pair in range(columns // LANES):
            head = group * n_context + 2 * pair
            lanes = slice(pair * LANES, (pair + 1) * LANES)
            for image in range(images):
                first = scratch[head, image].astype(f32)
                second = scratch[head + 1, image].astype(f32)
                start = image * rows
                here = slice(start, start + rows)
                grads[group, 0, here, lanes] = jnp.where(
                    low, first[:rows], swap(second[:rows])
                ).astype(bf16)
                grads[group, 1, here, lanes] = jnp.where(
                    low, swap(first[:rows]), second[:rows]
                ).astype(bf16)
                grads[group, 2, start : start + half, lanes] = jnp.where(
                    low_half, first[rows:], swap(second[rows:])
                ).astype(bf16)
                grads[group, 2, start + half : start + rows, lanes] = jnp.where(
                    low_half, swap(first[rows:]), second[rows:]
                ).astype(bf16)
    for group, ref in ((y, own_ref), (1 - y, far_ref)):
        for part in range(3):
            term = mm(grads[group, part], ref[:, part * columns : (part + 1) * columns], NT)
            total = term if total is None else total + term
    part_ref[...] = total.astype(bf16)


def head_grads_kernel(place_ref, *refs):
    pieces, (out_ref, wout_ref, scratch) = refs[:-3], refs[-3:]
    z = place_ref[1]
    count = len(pieces)
    rows = out_ref.shape[0]
    for j in range(count):
        head = lax.rem(z + j, count)
        for part in range(3):
            start = pl.multiple_of(part * count * HD + head * HD, HD)
            scratch[pl.ds(start, HD), :] = pieces[j][part * HD : (part + 1) * HD].astype(f32)
    out_ref[...] = jnp.transpose(scratch[...])[:rows]
    for block in range(wout_ref.shape[0] // LANES):
        lines = slice(3 * HD + block * rows, 3 * HD + (block + 1) * rows)
        total = pieces[0][lines].astype(f32)
        for piece in pieces[1:]:
            total = total + piece[lines].astype(f32)
        wout_ref[block * LANES : (block + 1) * LANES, :] = jnp.transpose(total)


def finish_kernel(
    sizes, place_ref, x_ref, middle_grad_ref, part_ref, other_ref, vec_ref, sums_ref, extra_ref,
    gup_ref, gqv_ref, out_ref, own_ref, far_ref,
):
    n_shard, n_context, last = sizes
    x, z = place_ref[0], place_ref[1]
    width = x_ref.shape[1]
    piece_rows = width // (n_shard * n_context)
    norm_grad = part_ref[...].astype(f32) + other_ref[...].astype(f32)
    normed, inv_std = normalise(x_ref[...].astype(f32))
    gain = vec_ref[GAIN1 : GAIN1 + 1, :]
    out_ref[...] = (
        middle_grad_ref[...] + norm_back(norm_grad * gain, normed, inv_std)
    ).astype(bf16)
    line = lax.broadcasted_iota(jnp.int32, sums_ref.shape, 0)
    sums = jnp.where(line == GAIN1, column_sum(norm_grad * normed), sums_ref[...])
    sums = jnp.where(line == SHIFT1, column_sum(norm_grad), sums)
    sums = jnp.where(line == SCALE2, extra_ref[0:1, :], sums).astype(bf16)
    up = gup_ref[...]
    line = lax.broadcasted_iota(jnp.int32, (SMALL_ROWS, up.shape[1]), 0)
    column = lax.broadcasted_iota(jnp.int32, (SMALL_ROWS, up.shape[1]), 1) // HD
    up = jnp.where(column == line, up, 0.0).astype(bf16)
    line = lax.broadcasted_iota(jnp.int32, (SMALL_ROWS, LANES), 0)
    low = low_lanes((SMALL_ROWS, LANES))
    qv = jnp.where((line == z) & low, gqv_ref[0:1, :], 0.0)
    qv = (qv + jnp.where((line == n_context + z) & low, gqv_ref[1:2, :], 0.0)).astype(bf16)
    for xr in range(n_shard):
        for zr in range(n_context):
            sc = lax.rem(x - xr + n_shard, n_shard) * n_context
            sc = sc + lax.rem(z - zr + n_context, n_context)
            start = (xr * n_context + zr) * SMALL_ROWS
            lines = slice(start, start + SMALL_ROWS)
            entry = lax.broadcasted_iota(jnp.int32, (LANES, width), 0)
            column = lax.broadcasted_iota(jnp.int32, (LANES, width), 1)
            place = jnp.where(
                (entry < piece_rows) & (column == sc * piece_rows + entry), 1.0, 0.0
            ).astype(bf16)
            term = mm(sums, place, NT)
            own_ref[lines, :LANES] = term
            far_ref[lines, :] = term
            own_ref[lines, LANES : 2 * LANES] = mm(up, spread_mask(sc, last, up.shape[1]), NT)
            own_ref[lines, 2 * LANES :] = mm(qv, spread_mask(sc, last, LANES), NT)


def merge_kernel(place_ref, own_ref, near_ref, far_ref, out_ref):
    y, core, image = place_ref[2], place_ref[3], pl.program_id(0)
    half = near_ref.shape[0]
    rows = own_ref.shape[0]
    block = rows // 2
    out_ref[0, pl.ds(pl.multiple_of(y * rows, 16), rows), :] = own_ref[...].astype(f32)
    for part in range(2):
        first = image * rows + part * block
        source = first // half
        line = pl.multiple_of(first - source * half, 16)
        there = pl.multiple_of((1 - y) * rows + part * block, 16)

        @pl.when(source == core)
        def _():
            out_ref[0, pl.ds(there, block), :] = near_ref[pl.ds(line, block), :].astype(f32)

        @pl.when(source != core)
        def _():
            out_ref[0, pl.ds(there, block), :] = far_ref[pl.ds(line, block), :].astype(f32)


KERNEL_US = {
    "bundle": 3,
    "prepare": 2,
    "attend": 26,
    "project": 4,
    "norm": 4,
    "mlp": 19,
    "mlp_weights": 12,
    "back": 8,
    "out_weights": 3,
    "result": 6,
    "attend_back": 26,
    "qkv_back": 6,
    "finish": 6,
    "head_grads": 2,
    "merge": 4,
}


def cost_of(name):
    time = KERNEL_US[name]
    return pl.CostEstimate(
        flops=int(time * FLOPS), transcendentals=0, bytes_accessed=int(time * BYTES)
    )


def vmem():
    return pl.BlockSpec(memory_space=pltpu.VMEM)


def smem():
    return pl.BlockSpec(memory_space=pltpu.SMEM)


def shaped(shape, dtype):
    return jax.ShapeDtypeStruct(shape, dtype)


def call(kernel, name, out_shape, scratch, place, *operands):
    return pl.pallas_call(
        kernel,
        name=name,
        cost_estimate=cost_of(name),
        in_specs=[smem()] + [vmem()] * len(operands),
        out_specs=[vmem()] * len(out_shape),
        out_shape=out_shape,
        scratch_shapes=scratch,
    )(place, *operands)


def per_device(sizes, *args):
    (
        tokens_in,
        counts,
        w_qkv,
        b_qv,
        w_out,
        b_out,
        w_up,
        b_up,
        w_down,
        b_down,
        norm1_gain,
        norm1_bias,
        norm2_gain,
        norm2_bias,
        scale1,
        scale2,
        cotangent,
    ) = args
    n_shard, n_context, n_y = sizes
    images, row_count, width = tokens_in.shape
    piece_rows = w_qkv.shape[0]
    head_columns = w_qkv.shape[2]
    hidden = w_up.shape[1]
    last = b_up.shape[1]
    rows = row_count // n_y
    half = rows // 2
    tokens = images * rows
    x = lax.axis_index("shard")
    z = lax.axis_index("context")
    y = lax.axis_index("y")
    core = lax.axis_index("core")
    place = jnp.stack([x, z, y, core]).astype(jnp.int32)
    blocks = n_y * n_context
    everyone = ("shard", "context")

    def send(value, axis, step):
        size = {"shard": n_shard, "context": n_context}[axis]
        return lax.ppermute(value, axis, [(i, (i + step) % size) for i in range(size)])

    def across(value):
        return lax.ppermute(value, "y", [(0, 1), (1, 0)])

    def partner(value):
        return lax.ppermute(value, "core", [(0, 1), (1, 0)])

    def hand_over(values, back):
        out = [values[0]]
        for slot in range(1, blocks):
            jy, jz = slot // n_context, slot % n_context
            step = -jz if back else jz
            pairs = [
                (i * n_y + t, (i + step) % n_context * n_y + (t ^ jy))
                for i in range(n_context)
                for t in range(n_y)
            ]
            out.append(lax.ppermute(values[slot], ("context", "y"), pairs))
        return out

    flat_qkv = w_qkv.reshape(piece_rows, -1)
    attention = lax.all_gather(
        jnp.concatenate([flat_qkv, w_out.T], axis=1), everyone, axis=0, tiled=True
    )
    feed = lax.all_gather(
        jnp.concatenate([w_up, w_down.T], axis=1), everyone, axis=0, tiled=True
    )

    vectors = [b_out, b_down, norm1_gain, norm1_bias, norm2_gain, norm2_bias, scale1, scale2]

    def block_of(value):
        return jnp.pad(value, ((0, SMALL_ROWS - value.shape[0]), (0, LANES - value.shape[1])))

    small = jnp.concatenate(
        [block_of(jnp.stack(vectors)), block_of(b_up), block_of(b_qv.reshape(-1, last))], axis=0
    )
    step_rows = piece_rows + 3 * SMALL_ROWS
    quarter_rows = half
    quarter = images * quarter_rows
    block = block_rows(step_rows)
    bundles = call(
        bundle_kernel,
        "bundle",
        [shaped((block, width), bf16)]
        + [shaped((quarter + block, width), bf16)] * (n_context - 1),
        [pltpu.VMEM((n_context, block, width), bf16)],
        place,
        flat_qkv,
        small,
        tokens_in,
    )
    near = [send(bundles[j], "context", j) for j in range(1, n_context)]
    head_stack = jnp.concatenate([bundles[0]] + [value[quarter:] for value in near], axis=0)
    head_stacks = [head_stack] + [send(head_stack, "shard", j) for j in range(1, n_shard)]
    def after(value, *others):
        return lax.optimization_barrier((value, *others))[0]

    weight_head, vec, bias_head, bup = call(
        functools.partial(prepare_kernel, (n_shard, n_context, last, b_qv.shape[1])),
        "prepare",
        [
            shaped((width, 2 * LANES), bf16),
            shaped((SMALL_ROWS, width), f32),
            shaped((8, 2 * LANES), f32),
            shaped((1, hidden), f32),
        ],
        [],
        place,
        *head_stacks,
    )

    fars = {}
    for j in sorted(range(n_context - 1), key=lambda j: min(j, n_context - 2 - j)):
        value = near[j][:quarter]
        if min(j, n_context - 2 - j):
            value = after(value, *fars.values())
        fars[j] = across(value)
    quarters = []
    for j, value in enumerate(near):
        value, far = value[:quarter], fars[j]
        crossed = after(far, weight_head) if j + 1 == n_context // 2 else far
        quarters += [value, far, partner(value), partner(crossed)]
    wout = attention[:, 3 * head_columns :]
    wout_far = across(after(wout, *quarters))
    def own_rows(array):
        return lax.dynamic_slice_in_dim(array, y * rows, rows, 1).reshape(tokens, width)

    residual = own_rows(tokens_in)
    upstream = own_rows(cotangent)

    pack_rows = rows + half
    slot = jnp.arange(blocks)
    source = (z - slot % n_context) % n_context * row_count + (y ^ (slot // n_context)) * rows
    key_place = (source[:, None] + jnp.arange(rows)[None, :]).reshape(1, -1).astype(jnp.int32)
    length = blocks * rows
    pack_spec = pl.BlockSpec((1, pack_rows, LANES), lambda i: (i, 0, 0))
    fold_spec = pl.BlockSpec((1, half, LANES), lambda i: (i, 0, 0))
    pos_spec = pl.BlockSpec((1, length), lambda i: (0, 0))
    log_spec = pl.BlockSpec((1, length, 1), lambda i: (i, 0, 0))
    head_spec = pl.BlockSpec((1, length, LANES), lambda i: (i, 0, 0))
    norm_spec = pl.BlockSpec((1, length, width), lambda i: (i, 0, 0))

    def fixed(shape):
        return pl.BlockSpec(shape, lambda i: (0,) * len(shape))

    attended = pl.pallas_call(
        functools.partial(attend_kernel, n_context),
        name="attend",
        cost_estimate=cost_of("attend"),
        grid=(images,),
        in_specs=[smem(), smem(), pos_spec]
        + [fixed((width, 2 * LANES)), fixed((SMALL_ROWS, width)), fixed((8, 2 * LANES))]
        + [pl.BlockSpec((1, row_count, width), lambda i: (i, 0, 0))]
        + [pl.BlockSpec((quarter_rows, width), lambda i: (i, 0))] * len(quarters),
        out_specs=[fold_spec] * blocks + [log_spec, norm_spec, head_spec, head_spec],
        out_shape=[shaped((images, half, LANES), bf16)] * blocks
        + [
            shaped((images, length, 1), f32),
            shaped((images, length, width), bf16),
            shaped((images, length, LANES), bf16),
            shaped((images, length, LANES), bf16),
        ],
        scratch_shapes=[pltpu.VMEM((length, LANES), bf16), pltpu.VMEM((rows, width), bf16)],
    )(counts, place, key_place, weight_head, vec, bias_head, tokens_in, *quarters)
    mixes, (log_total, norm_all, head_qk, head_v) = attended[:blocks], attended[blocks:]
    folded = hand_over(mixes, True)

    fold_scratch = pltpu.VMEM((blocks, images, half, LANES), bf16)
    mixture, proj_part = call(
        functools.partial(project_kernel, n_context),
        "project",
        [shaped((tokens, blocks * HD), bf16), shaped((tokens, width), bf16)],
        [fold_scratch],
        place,
        *folded,
        wout,
        wout_far,
    )
    proj_other = partner(proj_part)

    core_rows = tokens // CORES
    norm_own, norm_half = call(
        norm_kernel,
        "norm",
        [shaped((tokens, width), bf16), shaped((core_rows, width), bf16)],
        [],
        place,
        residual,
        proj_part,
        proj_other,
        vec,
    )
    norm_near = across(norm_half)
    norm_far = partner(norm_near)
    wqkv = after(attention[:, : 3 * head_columns], norm_near)
    wqkv_far = across(wqkv)
    mlp_rows = n_y * tokens
    (norm_low2, branch_grad, hidden_act, pre_grad, grad_bup, *halves) = call(
        mlp_kernel,
        "mlp",
        [
            shaped((mlp_rows, width), bf16),
            shaped((mlp_rows, width), bf16),
            shaped((mlp_rows, hidden), bf16),
            shaped((mlp_rows, hidden), bf16),
            shaped((1, hidden), f32),
        ]
        + [shaped((tokens, width), bf16)] * 4,
        [pltpu.VMEM((mlp_rows, width), bf16)],
        place,
        norm_own,
        norm_near,
        norm_far,
        cotangent,
        vec,
        bup,
        feed,
    )

    def sum_cores(mine, given):
        return (mine.astype(f32) + partner(given).astype(f32)).astype(bf16)

    def sum_y(both):
        part = both[:core_rows].astype(f32) + across(both[core_rows:]).astype(f32)
        return part.astype(bf16)

    back_both = sum_cores(halves[0], halves[1])
    back_half = sum_y(back_both)
    hidden_act = after(hidden_act, back_both)
    steps = 2
    columns = hidden // steps
    whole_spec = pl.BlockSpec((mlp_rows, width), lambda i, k: (0, 0))
    feed_grad = pl.pallas_call(
        mlp_weights_kernel,
        name="mlp_weights",
        cost_estimate=cost_of("mlp_weights"),
        grid=(2, steps),
        in_specs=[
            whole_spec,
            whole_spec,
            pl.BlockSpec((mlp_rows, columns), lambda i, k: (0, i * k)),
            pl.BlockSpec((mlp_rows, columns), lambda i, k: (0, (1 - i) * k + i * (steps - 1))),
        ],
        out_specs=pl.BlockSpec((width, columns), lambda i, k: (0, i * steps + k)),
        out_shape=shaped((width, 2 * hidden), bf16),
        scratch_shapes=[pltpu.VMEM((width, mlp_rows), bf16)] * 2,
    )(norm_low2, branch_grad, hidden_act, pre_grad)
    back_half, feed_grad = lax.optimization_barrier((back_half, feed_grad))
    back_far = partner(back_half)
    feed_grad = lax.psum_scatter(feed_grad, everyone, scatter_dimension=0, tiled=True)

    back = call(
        functools.partial(back_kernel, images, n_context),
        "back",
        [
            shaped((tokens, width), f32),
            shaped((tokens, width), bf16),
            shaped((SMALL_ROWS, width), f32),
        ]
        + [shaped((images, half, LANES), bf16)] * blocks,
        [fold_scratch, pltpu.VMEM((tokens, width), f32)],
        place,
        residual,
        upstream,
        proj_part,
        proj_other,
        back_half,
        back_far,
        vec,
        wout,
        wout_far,
    )
    middle_grad, proj_grad, sums = back[:3]
    mix_grads = hand_over(back[3:], False)
    out_own, out_far = call(
        out_weights_kernel,
        "out_weights",
        [shaped((width, head_columns), bf16)] * 2,
        [],
        place,
        proj_grad,
        mixture,
    )

    down_half = sum_y(sum_cores(after(halves[2], back_half), halves[3]))
    down_half = after(down_half, proj_grad)
    result, extra = call(
        result_kernel,
        "result",
        [shaped((tokens, width), bf16), shaped((8, width), f32)],
        [pltpu.VMEM((tokens, width), f32)],
        place,
        residual,
        upstream,
        proj_part,
        proj_other,
        down_half,
        partner(down_half),
        vec,
    )

    mix_grads = lax.optimization_barrier((out_own, out_far, result, extra, *mix_grads))
    out_own, out_far, result, extra = mix_grads[:4]
    mix_grads = mix_grads[4:]
    attended_back = pl.pallas_call(
        attend_back_kernel,
        name="attend_back",
        cost_estimate=cost_of("attend_back"),
        grid=(images,),
        in_specs=[smem(), pos_spec, log_spec, norm_spec, head_spec, head_spec]
        + [fold_spec] * (2 * blocks),
        out_specs=[pack_spec] * blocks + [fixed((3 * HD, width)), fixed((8, LANES))],
        out_shape=[shaped((images, pack_rows, LANES), bf16)] * blocks
        + [shaped((3 * HD, width), f32), shaped((8, LANES), f32)],
        scratch_shapes=[
            pltpu.VMEM((length, LANES), bf16),
            pltpu.VMEM((2 * HD, length), f32),
            pltpu.VMEM((length, LANES), f32),
            pltpu.VMEM((3 * HD, length), bf16),
        ],
    )(counts, key_place, log_total, norm_all, head_qk, head_v, *mixes, *mix_grads)
    grad_head, grad_qv = attended_back[blocks:]
    pack_grads = hand_over(attended_back[:blocks], True)

    part_rows = n_context * piece_rows
    def whole_rows(value):
        mine = lax.dynamic_slice_in_dim(value, core * (tokens // 2), tokens // 2, 0)
        near = across(mine)
        far = partner(near)
        half_spec = pl.BlockSpec((tokens // 2, width), lambda i: (0, 0))
        return pl.pallas_call(
            merge_kernel,
            name="merge",
        cost_estimate=cost_of("merge"),
            grid=(images,),
            in_specs=[smem(), pl.BlockSpec((rows, width), lambda i: (i, 0)), half_spec, half_spec],
            out_specs=pl.BlockSpec((1, row_count, width), lambda i: (i, 0, 0)),
            out_shape=shaped((images, row_count, width), f32),
        )(place, value, near, far)

    pack_grads = lax.optimization_barrier(
        (
            feed_grad[:, :hidden].astype(f32),
            feed_grad[:, hidden:].astype(f32).T,
            *pack_grads,
        )
    )
    grad_wup, grad_wdown = pack_grads[:2]
    pack_grads = pack_grads[2:]
    (norm1_part,) = call(
        functools.partial(qkv_back_kernel, n_context),
        "qkv_back",
        [shaped((tokens, width), bf16)],
        [
            pltpu.VMEM((blocks, images, pack_rows, LANES), bf16),
            pltpu.VMEM((n_y, 3, tokens, head_columns), bf16),
        ],
        place,
        *pack_grads,
        wqkv,
        wqkv_far,
    )
    norm1_other = partner(norm1_part)

    input_grad, own, far = call(
        functools.partial(finish_kernel, (n_shard, n_context, last)),
        "finish",
        [shaped((tokens, width), bf16)]
        + [
            shaped((n_shard * n_context * SMALL_ROWS, SMALL_LANES), f32),
            shaped((n_shard * n_context * SMALL_ROWS, LANES), f32),
        ],
        [],
        place,
        residual,
        middle_grad,
        norm1_part,
        norm1_other,
        vec,
        sums,
        extra,
        grad_bup,
        grad_qv,
    )
    far = jnp.pad(across(far), ((0, 0), (0, SMALL_LANES - LANES)))
    total = (own + far).reshape(n_shard, -1, SMALL_LANES)
    over_shard = total[0]
    for j in range(1, n_shard):
        over_shard = over_shard + send(total[j], "shard", -j)
    over_shard = over_shard.reshape(n_context, SMALL_ROWS, SMALL_LANES)
    small_grad = over_shard[0]
    for j in range(1, n_context):
        small_grad = small_grad + send(over_shard[j], "context", -j)

    out_sum = (out_own.astype(f32) + across(out_far).astype(f32)).astype(bf16)
    grad_head, out_sum = lax.optimization_barrier(
        (grad_head, out_sum, norm1_part)
    )[:2]

    def shard_part(j):
        start = lax.rem(x - j + n_shard, n_shard) * part_rows
        head = lax.dynamic_slice_in_dim(grad_head, start, part_rows, 1).astype(bf16)
        rest = lax.dynamic_slice_in_dim(out_sum, start, part_rows, 0)
        wide = part_rows // head_columns
        if wide > 1:
            rest = jnp.concatenate(jnp.split(rest, wide, axis=0), axis=1)
        else:
            rest = jnp.concatenate(jnp.split(rest, head_columns // part_rows, axis=1), axis=0)
        return jnp.concatenate([head, rest], axis=0)

    both = shard_part(0).astype(f32)
    for j in range(1, n_shard):
        both = both + send(shard_part(j), "shard", -j).astype(f32)
    both = after(both.astype(bf16), input_grad)
    head_sum, out_sum = both[: 3 * HD], both[3 * HD :]
    if part_rows > head_columns:
        out_sum = jnp.concatenate(jnp.split(out_sum, part_rows // head_columns, axis=1), axis=0)
    else:
        out_sum = jnp.concatenate(jnp.split(out_sum, head_columns // part_rows, axis=0), axis=1)
    lane_pad = -piece_rows % LANES

    def context_part(j):
        start = lax.rem(z - j + n_context, n_context) * piece_rows
        head = lax.dynamic_slice_in_dim(head_sum, start, piece_rows, 1)
        rest = lax.dynamic_slice_in_dim(out_sum, start, piece_rows, 0)
        rest = jnp.concatenate(jnp.split(rest, head_columns // LANES, axis=1), axis=0)
        return jnp.concatenate([jnp.pad(head, ((0, 0), (0, lane_pad))), rest], axis=0)

    parts = [context_part(0)]
    for j in range(1, n_context):
        parts.append(send(context_part(j), "context", -j))
    grad_wqkv, grad_wout = call(
        head_grads_kernel,
        "head_grads",
        [shaped((piece_rows, 3 * head_columns), f32), shaped((head_columns, piece_rows), f32)],
        [pltpu.VMEM((3 * head_columns, piece_rows + lane_pad), f32)],
        place,
        *parts,
    )
    vec_grad = small_grad[: len(vectors), :piece_rows]
    return (
        whole_rows(result),
        whole_rows(input_grad),
        grad_wqkv.reshape(piece_rows, 3, head_columns),
        small_grad[: b_qv.shape[0] * b_qv.shape[1], 2 * LANES : 2 * LANES + last].reshape(
            b_qv.shape
        ),
        grad_wout,
        vec_grad[B_OUT],
        grad_wup,
        small_grad[: b_up.shape[0], LANES : LANES + last],
        grad_wdown,
        vec_grad[B_DOWN],
        vec_grad[GAIN1],
        vec_grad[SHIFT1],
        vec_grad[GAIN2],
        vec_grad[SHIFT2],
        vec_grad[SCALE1],
        vec_grad[SCALE2],
    )


def solution(mesh):
    pair = ("y", "core")
    both = ("shard", "context")
    tokens = P("shard", "context", None)
    vector = P(both)
    in_specs = (
        tokens,
        P("shard"),
        P(both, None, pair),
        P(None, pair, both),
        P(pair, both),
        vector,
        P(both, pair),
        P(pair, both),
        P(pair, both),
    ) + (vector,) * 7
    in_specs = in_specs + (tokens,)
    out_specs = (
        tokens,
        tokens,
        P(both, None, pair),
        P(None, pair, both),
        P(pair, both),
        vector,
        P(both, pair),
        P(pair, both),
        P(pair, both),
    ) + (vector,) * 7
    sizes = tuple(mesh.shape[name] for name in ("shard", "context", "tensor"))
    split = Mesh(
        mesh.devices.reshape(sizes[0], sizes[1], sizes[2] // CORES, CORES),
        ("shard", "context", "y", "core"),
    )
    return jax.shard_map(
        functools.partial(per_device, split.devices.shape[:3]),
        mesh=split,
        in_specs=in_specs,
        out_specs=out_specs,
        check_vma=False,
    )
```
